128 devices in a mesh: rad: 8 (over y, core), ang: 16 (over x, z).
Axes of the slice: x: 4, y: 4, z: 4, core: 2. Of those that a mesh axis runs over, the one named last changes fastest.
Arguments:
- source_coeffs: bfloat16 [512, 512, 2, 128], P('ang', 'rad'), may hold values from -6 to 6
- inverses: bfloat16 [512, 128, 128], P('rad')
- velocity: bfloat16 [2, 768, 128, 1536], P(None, 'ang', 'rad'), may hold values from -6 to 6
- order_slots: int32 [512], replicated, may hold values from 0 to 511, as said below
Outputs:
- advected: bfloat16 [512, 2, 128, 512], P('ang', None, 'rad')
The draws below stay inside these ranges and needn't reach their ends.
Inputs may be any that keep to these rules, and one draw needn't show every extreme that they name: `order_slots`: the slots form 512 // 32 consecutive blocks of 32; in each block the first 16 slots hold distinct orders below 256, and slot 16 + i of a block holds 511 minus the order in slot i of that block; every order appears exactly once.
All inputs are finite; a program needn't handle non-finite values.
Results may differ from the reference program's by a relative error of at most 0.012.
Values may be sent and summed in bfloat16 or wider, within the bound.
No kernel may reach another device: no remote copies, remote signals or barrier semaphores. Data moves between devices by JAX's collectives and lax.ppermute only.
A program may use at most 256 MiB of HBM per device.

```python
import math
import jax
import jax.numpy as jnp
from jax import lax

LMAX = 512
NLAT = 768
NLON = 1536
NR = 128
K = 128
PAIRS = 16


def draw_inverses(key, part):
    first_key, second_key = jax.random.split(jax.random.fold_in(key, 11))
    degree_values = jnp.arange(LMAX, dtype=jnp.float32)
    mode_values = jnp.arange(K, dtype=jnp.float32)
    mixing = jax.random.normal(first_key, (LMAX, K, K), jnp.float32)
    jitter = jax.random.uniform(second_key, (LMAX, K), jnp.float32, 0.5, 2.0)
    core_matrix = jnp.eye(K, dtype=jnp.float32)[None] * jitter[:, :, None] + 0.6 * mixing / jnp.sqrt(K * 1.0)
    decay = 4.0 / ((degree_values + 1.0)[:, None, None] * ((1.0 + mode_values) ** 1.5)[None, :, None])
    return (core_matrix * decay).astype(jnp.bfloat16)


def draw_order_slots(key, part):
    lower_orders = jax.random.permutation(jax.random.fold_in(key, 23), LMAX // 2).astype(jnp.int32)
    grouped = lower_orders.reshape(LMAX // (2 * PAIRS), PAIRS)
    paired = jnp.concatenate([grouped, LMAX - 1 - grouped], 1)
    return paired.reshape(LMAX)


def level_of(rng, dims, cuts, low, high):
    loudness, own = 1.0, jax.random.fold_in(rng, 6)
    for dim, blocks in cuts:
        draws = jnp.exp(jax.random.uniform(jax.random.fold_in(own, dim), (blocks,), jnp.float32, low / len(cuts), high / len(cuts)))
        loudness = loudness * jnp.repeat(draws, dims[dim] // blocks).reshape([-1 if axis == dim else 1 for axis in range(len(dims))])
    return loudness


def bell_draw(rng, shape, scale, reach, cuts=(), held_as=jnp.bfloat16):
    drawn = jax.random.normal(rng, shape, jnp.float32) * scale
    if len(cuts) > 0:
        drawn = level_of(rng, shape, cuts, -0.22, 0.18) * drawn
    return jnp.clip(drawn, min=-reach, max=reach).astype(held_as)


def setup_inputs(seed: int = 0) -> dict:
    splits = jax.random.split(jax.random.key(seed), 5)
    return {
        "source_coeffs": bell_draw(splits[0], (LMAX, LMAX, 2, K), 1.0, 6.0, ((0, 16), (1, 8))),
        "inverses": draw_inverses(jax.random.fold_in(splits[4], 71), 0),
        "velocity": bell_draw(splits[2], (2, NLAT, NR, NLON), 1.0, 6.0, ((1, 16), (2, 8))),
        "order_slots": draw_order_slots(jax.random.fold_in(splits[4], 71), 0),
    }


inner_radius = 0.35
rescale_bound = 1e+20
rescale_log = 46.051701859880914
start_log = -1.2051210046670229

def round_keep(array_in):
    return lax.optimization_barrier(array_in.astype(jnp.bfloat16)).astype(jnp.float32)

def legendre_rows(orders, degree_count, lat_count):
    colatitude = (jnp.arange(lat_count, dtype=jnp.float32) + 0.5) * (math.pi / lat_count)
    cosines = jnp.cos(colatitude)[None, :]
    sines = jnp.sin(colatitude)[None, :]
    order_value = orders.astype(jnp.float32)[:, None]
    orders_col = orders.astype(jnp.int32)[:, None]
    log_start = start_log + 0.5 * (lax.lgamma(order_value + 1.5) - lax.lgamma(order_value + 1.0)) + order_value * jnp.log(sines)
    zero_field = jnp.zeros((orders.shape[0], lat_count), jnp.float32)

    def advance(state_carry, degree):
        prev_one, prev_two, log_scale = state_carry
        degree_value = degree.astype(jnp.float32)
        denominator = jnp.maximum(degree_value * degree_value - order_value * order_value, 1.0)
        recur_a = jnp.sqrt(jnp.maximum(4.0 * degree_value * degree_value - 1.0, 1.0) / denominator)
        lower_sq = (degree_value - 1.0) * (degree_value - 1.0)
        recur_b = jnp.sqrt(jnp.maximum(lower_sq - order_value * order_value, 0.0) / jnp.maximum(4.0 * lower_sq - 1.0, 1.0))
        grown_value = recur_a * (cosines * prev_one - recur_b * prev_two)
        before = degree < orders_col
        starting = degree == orders_col
        current = jnp.where(before, 0.0, jnp.where(starting, 1.0, grown_value))
        previous = jnp.where(before | starting, 0.0, prev_one)
        too_large = jnp.abs(current) > rescale_bound
        factor = jnp.where(too_large, 1.0 / rescale_bound, 1.0)
        log_scale = log_scale + jnp.where(too_large, rescale_log, 0.0)
        current = current * factor
        previous = previous * factor
        value_scaled = current * jnp.exp(log_scale)
        return ((current, previous, log_scale), value_scaled.astype(jnp.bfloat16))
    _, legendre = lax.scan(advance, (zero_field, zero_field, log_start + zero_field), jnp.arange(degree_count, dtype=jnp.int32))
    return legendre

def radial_tables(mode_count, radius_count):
    angles = (jnp.arange(radius_count, dtype=jnp.float32) + 0.5) * (math.pi / radius_count)
    mode_values = jnp.arange(mode_count, dtype=jnp.float32)[:, None]
    values = jnp.cos(mode_values * angles[None, :])
    slopes = mode_values * jnp.sin(mode_values * angles[None, :]) / jnp.sin(angles)[None, :] * (2.0 / (1.0 - inner_radius))
    return jnp.stack([values, slopes])

def fourier_tables(orders, lon_count):
    phase_index = orders.astype(jnp.int32)[:, None] * jnp.arange(lon_count, dtype=jnp.int32)[None, :] % lon_count
    phase_angle = phase_index.astype(jnp.float32) * (2.0 * math.pi / lon_count)
    weight = jnp.where(orders == 0, 1.0, 2.0).astype(jnp.float32)[:, None]
    cosine = jnp.cos(phase_angle)
    sine = jnp.sin(phase_angle)
    synth_table = jnp.stack([weight * cosine, -weight * sine], 1).astype(jnp.bfloat16)
    analyse_table = (jnp.stack([cosine, -sine], 1) * (2.0 * math.pi / lon_count)).astype(jnp.bfloat16)
    return (synth_table, analyse_table)

def reference(source_coeffs, inverses, velocity, order_slots):
    slot_count, degree_count, _, mode_count = source_coeffs.shape
    lat_count = velocity.shape[1]
    radius_count = velocity.shape[2]
    lon_count = velocity.shape[3]
    degrees = jnp.arange(degree_count, dtype=jnp.int32)
    degree_mask = (degrees[None, :] >= order_slots[:, None]).astype(jnp.float32)
    solved = jnp.einsum('lkj,slcj->slck', inverses.astype(jnp.float32), source_coeffs.astype(jnp.float32), precision=lax.Precision.HIGHEST) * degree_mask[:, :, None, None]
    tables = radial_tables(mode_count, radius_count)
    synth_table, analyse_table = fourier_tables(order_slots, lon_count)
    colatitude = (jnp.arange(lat_count, dtype=jnp.float32) + 0.5) * (math.pi / lat_count)
    sines = jnp.sin(colatitude)
    quad_weight = math.pi / lat_count * sines
    angles = (jnp.arange(radius_count, dtype=jnp.float32) + 0.5) * (math.pi / radius_count)
    radius_values = inner_radius + (1.0 - inner_radius) * (jnp.cos(angles) + 1.0) * 0.5
    order_value = order_slots.astype(jnp.float32)
    block_size = min(32, slot_count)
    slot_blocks = slot_count // block_size
    radius_block = min(16, radius_count)
    radius_blocks = radius_count // radius_block

    def radius_piece(start):
        table_piece = lax.dynamic_slice_in_dim(tables, start, radius_block, 2)
        radius_local = lax.dynamic_slice_in_dim(radius_values, start, radius_block, 0)
        velocity_piece = lax.dynamic_slice_in_dim(velocity, start, radius_block, 2).astype(jnp.float32)

        def synth_block(slot_block):
            first_slot = slot_block * block_size
            orders = lax.dynamic_slice_in_dim(order_slots, first_slot, block_size, 0)
            legendre = legendre_rows(orders, degree_count, lat_count).astype(jnp.float32)
            solved_piece = lax.dynamic_slice_in_dim(solved, first_slot, block_size, 0)
            radial = round_keep(jnp.einsum('slck,fki->sfcli', solved_piece, table_piece, precision=lax.Precision.HIGHEST))
            lat_spec = round_keep(jnp.einsum('sfcli,lsj->sfcij', radial, legendre))
            order_piece = lax.dynamic_slice_in_dim(order_value, first_slot, block_size, 0)[:, None, None]
            azim = jnp.stack([-order_piece * lat_spec[:, 0, 1], order_piece * lat_spec[:, 0, 0]], 1)
            azim = round_keep(azim)
            return jnp.concatenate([lat_spec, azim[:, None]], 1)
        fields = lax.map(synth_block, jnp.arange(slot_blocks)).reshape(slot_count, 3, 2, radius_block, lat_count)
        physical = jnp.einsum('sfcij,scn->fjin', fields, synth_table.astype(jnp.float32))
        radius_col = radius_local[None, :, None]
        flux_term = velocity_piece[0] * (physical[1] + 3.0 * physical[0] / radius_col) + velocity_piece[1] * physical[2] / (radius_col * sines[:, None, None])
        flux_term = round_keep(flux_term)
        fourier = jnp.einsum('jin,scn->scij', flux_term, analyse_table.astype(jnp.float32))
        fourier = round_keep(fourier * quad_weight[None, None, None, :])

        def analyse_block(slot_block):
            first_slot = slot_block * block_size
            orders = lax.dynamic_slice_in_dim(order_slots, first_slot, block_size, 0)
            legendre = legendre_rows(orders, degree_count, lat_count).astype(jnp.float32)
            fourier_piece = lax.dynamic_slice_in_dim(fourier, first_slot, block_size, 0)
            return jnp.einsum('scij,lsj->scil', fourier_piece, legendre).astype(jnp.bfloat16)
        return lax.map(analyse_block, jnp.arange(slot_blocks)).reshape(slot_count, 2, radius_block, degree_count)
    pieces = lax.map(radius_piece, jnp.arange(radius_blocks, dtype=jnp.int32) * radius_block)
    return pieces.transpose(1, 2, 0, 3, 4).reshape(slot_count, 2, radius_count, degree_count)
```

```python
import math

import jax
import jax.numpy as jnp
import numpy as np
from jax import lax
from jax.experimental import pallas as pl
from jax.experimental.pallas import tpu as pltpu
from jax.sharding import PartitionSpec as P

f32 = jnp.float32
bf16 = jnp.bfloat16
inner_radius = 0.35
grow_bound = 1e10
grow_log = 23.025850929940457
start_log = -1.2051210046670229
vmem_bytes = 60 * 1024 * 1024

LMAX, NLAT, NLON, NR, K = 512, 768, 1536, 128, 128
HALF = NLAT // 2
NH = NLON // 2
NT = (((1,), (1,)), ((), ()))
TN = (((0,), (0,)), ((), ()))


def radial_matrix():
    u = (np.arange(NR) + 0.5) * (math.pi / NR)
    k = np.arange(K)[:, None]
    r = inner_radius + (1.0 - inner_radius) * (np.cos(u) + 1.0) * 0.5
    value = np.cos(k * u[None])
    slope = k * np.sin(k * u[None]) / np.sin(u)[None] * (2.0 / (1.0 - inner_radius))
    both = np.stack([value / r, slope + 3.0 * value / r], 0)
    both = both.reshape(2, K, 8, 16).transpose(1, 2, 0, 3).reshape(K, 256)
    out = np.zeros((2, K, 2, 256))
    out[0, :, 0] = both
    out[1, :, 1] = both
    return jnp.asarray(out.reshape(256, 512), f32).astype(bf16)


def params(sem=("arbitrary",)):
    return pltpu.CompilerParams(dimension_semantics=sem, vmem_limit_bytes=vmem_bytes)


def swap_chunks(x0, x1, x2, x3):
    lane = lax.broadcasted_iota(jnp.int32, x0.shape, 1)
    low = lane < 64
    even = (lane // 32) % 2 == 0
    a0 = jnp.where(low, x0, pltpu.roll(x2, 64, 1))
    a2 = jnp.where(low, pltpu.roll(x0, 64, 1), x2)
    a1 = jnp.where(low, x1, pltpu.roll(x3, 64, 1))
    a3 = jnp.where(low, pltpu.roll(x1, 64, 1), x3)
    y0 = jnp.where(even, a0, pltpu.roll(a1, 32, 1))
    y1 = jnp.where(even, pltpu.roll(a0, 96, 1), a1)
    y2 = jnp.where(even, a2, pltpu.roll(a3, 32, 1))
    y3 = jnp.where(even, pltpu.roll(a2, 96, 1), a3)
    return (y0, y1, y2, y3)


def solve_kernel(base_ref, src_ref, inv_ref, order_ref, out_ref, wide, acc):
    step = pl.program_id(0)
    steps = pl.num_programs(0)
    block = inv_ref.shape[0]

    @pl.when(step == 0)
    def _():
        def widen(s, _):
            wide[pl.ds(pl.multiple_of(s * 128, 128), 128), :] = src_ref[s].astype(f32)
            return 0

        lax.fori_loop(0, 32, widen, 0, unroll=4)

    order = order_ref[...]

    def degree(i, _):
        row = step * block + i
        x0 = wide[pl.ds(2 * row, 32, stride=128), :]
        x1 = wide[pl.ds(2 * row + 1, 32, stride=128), :]
        x = jnp.concatenate([x0, x1], 0).astype(bf16)
        y = lax.dot_general(x, inv_ref[i], NT, preferred_element_type=f32)
        y = jnp.where(order <= base_ref[0] + row, y, 0.0)
        acc[pl.ds(row, 64, stride=64), :] = y
        return 0

    lax.fori_loop(0, block, degree, 0, unroll=8)

    @pl.when(step == steps - 1)
    def _():
        for r in range(8):
            for lu in range(2):
                for q in range(2):
                    for c in range(2):
                        plane = c * 32 + lu * 16 + 2 * r + q
                        row = (lu * 4 + q * 2 + c) * 64
                        out_ref[r, row : row + 64, :] = acc[plane * 64 : plane * 64 + 64, :].astype(bf16)


def solve(source, inverses, orders, rad_index):
    src = source.reshape(32, 128, 128)
    order = jnp.broadcast_to(jnp.tile(orders, 2)[:, None], (64, 128))
    return pl.pallas_call(
        solve_kernel,
        grid_spec=pltpu.PrefetchScalarGridSpec(
            num_scalar_prefetch=1,
            grid=(4,),
            in_specs=[
                pl.BlockSpec((32, 128, 128), lambda g, b: (0, 0, 0)),
                pl.BlockSpec((16, 128, 128), lambda g, b: (g, 0, 0)),
                pl.BlockSpec((64, 128), lambda g, b: (0, 0)),
            ],
            out_specs=pl.BlockSpec((8, 512, 128), lambda g, b: (0, 0, 0)),
            scratch_shapes=[pltpu.VMEM((4096, 128), f32), pltpu.VMEM((4096, 128), f32)],
        ),
        out_shape=jax.ShapeDtypeStruct((8, 512, 128), bf16),
        compiler_params=params(),
        cost_estimate=pl.CostEstimate(flops=134217728, bytes_accessed=4194304, transcendentals=0),
        name="solve",
    )(jnp.reshape(rad_index * 64, (1,)), src, inverses, order)


def legendre_kernel(c1_ref, c2_ref, m_ref, x_ref, log_ref, low_ref, up_ref, p1, p2, lg, bp, tile):
    step = pl.program_id(0)

    @pl.when(step == 0)
    def _():
        p1[...] = jnp.zeros(p1.shape, f32)
        p2[...] = jnp.zeros(p2.shape, f32)
        bp[...] = jnp.zeros(bp.shape, f32)
        lg[...] = log_ref[...]

    def run(half, out_ref):
        rows = slice(half * 16, half * 16 + 16)
        m = m_ref[rows, :]
        m2 = m * m
        lanes = [slice(128 * t, 128 * t + 128) for t in range(3)]

        def sub(b, state):
            cur, prev, logs, below = state
            scale = [jnp.exp(v) for v in logs]
            for i in range(8):
                local = b * 8 + i
                l = step * 32 + local
                lf = l.astype(f32)
                d = jnp.maximum(lf * lf - m2, 1.0)
                r = lax.rsqrt(d)
                r = r * (1.5 - 0.5 * d * r * r)
                a = c1_ref[l] * r
                ab = a * below
                below = d * r * c2_ref[l]
                seed = jnp.where(m == lf, 1.0, 0.0)
                for t in range(3):
                    new = (a * x_ref[:, lanes[t]]) * cur[t] - ab * prev[t] + seed
                    prev[t] = cur[t]
                    cur[t] = new
                    tile[t, pl.ds(local, 16, stride=32), :] = new * scale[t]
            for t in range(3):
                big = jnp.abs(cur[t]) > grow_bound
                factor = jnp.where(big, 1.0 / grow_bound, 1.0)
                cur[t] = cur[t] * factor
                prev[t] = prev[t] * factor
                logs[t] = logs[t] + jnp.where(big, grow_log, 0.0)
            return (cur, prev, logs, below)

        state = (
            [p1[rows, v] for v in lanes],
            [p2[rows, v] for v in lanes],
            [lg[rows, v] for v in lanes],
            bp[rows, :],
        )
        cur, prev, logs, below = lax.fori_loop(0, 4, sub, state)
        for t in range(3):
            p1[rows, lanes[t]] = cur[t]
            p2[rows, lanes[t]] = prev[t]
            lg[rows, lanes[t]] = logs[t]
        bp[rows, :] = below
        for s in range(16):
            for t in range(3):
                out_ref[s, :, lanes[t]] = tile[t, s * 32 : s * 32 + 32, :].astype(bf16)

    run(0, low_ref)

    @pl.when(step >= 8)
    def _():
        run(1, up_ref)


def legendre_tables(orders):
    l = np.arange(LMAX, dtype=np.float64)
    root = np.sqrt(np.maximum(4.0 * l * l - 1.0, 1.0))
    t = (np.arange(HALF) + 0.5) * (math.pi / NLAT)
    gammas = [0.5 * (math.lgamma(m + 1.5) - math.lgamma(m + 1.0)) + start_log for m in range(LMAX)]
    x = jnp.asarray(np.broadcast_to(np.cos(t), (16, HALF)), f32)
    mf = orders.astype(f32)
    logs = jnp.take(jnp.asarray(gammas, f32), orders)[:, None] + mf[:, None] * jnp.asarray(np.log(np.sin(t)), f32)[None]
    return pl.pallas_call(
        legendre_kernel,
        grid_spec=pltpu.PrefetchScalarGridSpec(
            num_scalar_prefetch=2,
            grid=(16,),
            in_specs=[
                pl.BlockSpec((32, 128), lambda g, *_: (0, 0)),
                pl.BlockSpec((16, HALF), lambda g, *_: (0, 0)),
                pl.BlockSpec((32, HALF), lambda g, *_: (0, 0)),
            ],
            out_specs=[
                pl.BlockSpec((16, 32, HALF), lambda g, *_: (0, g, 0)),
                pl.BlockSpec((16, 32, HALF), lambda g, *_: (0, jnp.maximum(g - 8, 0), 0)),
            ],
            scratch_shapes=[
                pltpu.VMEM((32, HALF), f32),
                pltpu.VMEM((32, HALF), f32),
                pltpu.VMEM((32, HALF), f32),
                pltpu.VMEM((32, 128), f32),
                pltpu.VMEM((3, 512, 128), f32),
            ],
        ),
        out_shape=[
            jax.ShapeDtypeStruct((16, LMAX, HALF), bf16),
            jax.ShapeDtypeStruct((16, LMAX // 2, HALF), bf16),
        ],
        compiler_params=params(),
        cost_estimate=pl.CostEstimate(flops=60000000, bytes_accessed=12582912, transcendentals=100000),
        name="legendre",
    )(
        jnp.asarray(root, f32),
        jnp.asarray(1.0 / root, f32),
        jnp.broadcast_to(mf[:, None], (32, 128)),
        x,
        logs,
    )


def phase_rows(orders):
    m = jnp.repeat(orders, 2)[:, None]
    c = jnp.tile(jnp.asarray([0, NLON // 4], jnp.int32), orders.shape[0])[:, None]
    near = (m * jnp.arange(128, dtype=jnp.int32)[None] + c) % NLON
    far = (m * (128 * jnp.arange(8, dtype=jnp.int32))[None]) % NLON
    near = near.astype(f32) * (2.0 * math.pi / NLON)
    far = far.astype(f32) * (2.0 * math.pi / NLON)
    return (jnp.cos(near), jnp.sin(near), jnp.cos(far), jnp.sin(far))


def table_kernel(nc, ns, fc, fs, w, mw, anc, ans, afc, afs, t_ref, d_ref, a_ref):
    scale = (2.0 * math.pi / NLON) * (math.pi / NLAT)
    for b in range(6):
        lanes = slice(128 * b, 128 * b + 128)
        cosine = fc[:, b : b + 1] * nc[...] - fs[:, b : b + 1] * ns[...]
        sine = fs[:, b : b + 1] * nc[...] + fc[:, b : b + 1] * ns[...]
        t_ref[:, lanes] = (w[...] * cosine).astype(bf16)
        d_ref[:, lanes] = (mw[...] * sine).astype(bf16)
        a_ref[:, lanes] = (scale * (afc[:, b : b + 1] * anc[...] - afs[:, b : b + 1] * ans[...])).astype(bf16)


def fourier_tables(synth_orders, analyse_orders):
    synth = phase_rows(synth_orders)
    analyse = phase_rows(analyse_orders)
    m = jnp.repeat(synth_orders, 2).astype(f32)
    w = jnp.where(m == 0.0, 1.0, 2.0)
    w2 = jnp.broadcast_to(w[:, None], (1024, 128))
    mw2 = jnp.broadcast_to((-m * w)[:, None], (1024, 128))
    near = pl.BlockSpec((256, 128), lambda g: (g, 0))
    far = pl.BlockSpec((256, 8), lambda g: (g, 0))
    out = pl.BlockSpec((256, NH), lambda g: (g, 0))
    return pl.pallas_call(
        table_kernel,
        grid=(4,),
        in_specs=[near, near, far, far, near, near, near, near, far, far],
        out_specs=[out, out, out],
        out_shape=[jax.ShapeDtypeStruct((1024, NH), bf16)] * 3,
        compiler_params=params(),
        cost_estimate=pl.CostEstimate(flops=8000000, bytes_accessed=8000000, transcendentals=0),
        name="tables",
    )(*synth, w2, mw2, *analyse)


def synth_kernel(ints_ref, recv_ref, low_ref, up_ref, mat_ref, out_ref, ns, scr):
    mat = mat_ref[...]
    for lu in range(2):
        for q in range(2):
            first = 4 * lu
            count = 64 * (8 - first)
            h = ints_ref[1 + q]
            h = h if lu == 0 else 1 - h
            planes = []
            for c in range(2):
                row = (lu * 4 + q * 2 + c) * 64
                planes.append(recv_ref[first:8, row : row + 64, :].reshape(count, 128))
            coeffs = jnp.concatenate(planes, 1)
            rad = jnp.dot(coeffs, mat, preferred_element_type=f32)
            degree = lax.broadcasted_iota(jnp.int32, rad.shape, 0)
            sign = (1 - 2 * ((degree + h) % 2)).astype(f32)
            both = jnp.concatenate([rad.astype(bf16), (rad * sign).astype(bf16)], 1)
            table = low_ref[q] if lu == 0 else up_ref[q]
            wave = lax.dot_general(table, both, TN, preferred_element_type=f32)
            for tile in range(8):
                ns[tile] = wave[:, 128 * tile : 128 * tile + 128]
            for half in range(2):
                for c in range(2):
                    for rh in range(2):
                        tile = half * 4 + c * 2 + rh
                        parts = swap_chunks(*[ns[tile, pl.ds(j, 96, stride=4), :] for j in range(4)])
                        for rl in range(4):
                            base = (((rh * 4 + rl) * 2 + half) * 96) * 8 + q * 2 + c
                            scr[pl.ds(base + h * 4, 96, stride=8), :] = parts[rl]

    def emit(i, _):
        r = i // 16
        a = i % 16
        half = a // 8
        north = jnp.where(half == 0, a, 15 - a)
        start = pl.multiple_of(((r * 2 + half) * 96 + north * 12) * 8, 32)
        out_ref[i] = scr[pl.ds(start, 96), :].astype(bf16)
        return 0

    lax.fori_loop(0, 128, emit, 0, unroll=2)


def synth(recv, low, up, ints):
    return pl.pallas_call(
        synth_kernel,
        grid_spec=pltpu.PrefetchScalarGridSpec(
            num_scalar_prefetch=1,
            grid=(1,),
            in_specs=[
                pl.BlockSpec((8, 512, 128), lambda g, b: (0, 0, 0)),
                pl.BlockSpec((2, LMAX, HALF), lambda g, b: (b[0], 0, 0)),
                pl.BlockSpec((2, LMAX // 2, HALF), lambda g, b: (b[0], 0, 0)),
                pl.BlockSpec((256, 512), lambda g, b: (0, 0)),
            ],
            out_specs=pl.BlockSpec((128, 96, 128), lambda g, b: (0, 0, 0)),
            scratch_shapes=[pltpu.VMEM((8, HALF, 128), f32), pltpu.VMEM((8 * 2 * 96 * 8, 128), f32)],
        ),
        out_shape=jax.ShapeDtypeStruct((128, 96, 128), bf16),
        compiler_params=params(),
        cost_estimate=pl.CostEstimate(flops=2000000000, bytes_accessed=7000000, transcendentals=0),
        name="synth",
    )(ints, recv, low, up, radial_matrix())


def grid_kernel(
    ints_ref, sines_ref, recv_ref, vel_ref, t_ref, d_ref, a_ref, out_ref,
    ke, ko, l0e, l0o, l1e, l1o, se, so, ze, zo, ue, uo, oe, oo,
):
    step = pl.program_id(0)
    top = lax.broadcasted_iota(jnp.int32, (8, 128), 0) < 4

    def gather(u, _):
        a = recv_ref[2 * u].astype(f32)
        b = recv_ref[2 * u + 1].astype(f32)
        for t in range(4):
            at = a[8 * t : 8 * t + 8]
            bt = b[8 * t : 8 * t + 8]
            row = pl.multiple_of(t * 512 + 8 * u, 8)
            ke[pl.ds(row, 8), :] = jnp.where(top, at, pltpu.roll(bt, 4, 0))
            ko[pl.ds(row, 8), :] = jnp.where(top, pltpu.roll(at, 4, 0), bt)
        return 0

    lax.fori_loop(0, 64, gather, 0, unroll=4)
    for t in range(4):
        for src, zero, one in ((ke, l0e, l1e), (ko, l0o, l1o)):
            turned = src[512 * t : 512 * t + 512, :].T.astype(bf16)
            for j in range(4):
                row = (t * 4 + j) * 16
                zero[row : row + 16, :] = turned[32 * j : 32 * j + 16]
                one[row : row + 16, :] = turned[32 * j + 16 : 32 * j + 32]
    se[...] = jnp.dot(l1e[...], t_ref[0:512, :], preferred_element_type=f32)
    so[...] = jnp.dot(l1o[...], t_ref[512:1024, :], preferred_element_type=f32)
    ze[...] = jnp.dot(l0e[...], d_ref[0:512, :], preferred_element_type=f32)
    zo[...] = jnp.dot(l0o[...], d_ref[512:1024, :], preferred_element_type=f32)
    south = ints_ref[3]

    def flux(j, _):
        local = jnp.where(south == 1, 15 - j, j)
        sine = sines_ref[step * 16 + j]
        rows = pl.ds(pl.multiple_of(j * 16, 16), 16)
        for b in range(3):
            lo = slice(256 * b, 256 * b + 256)
            hi = slice(NH + 256 * b, NH + 256 * b + 256)
            v0 = vel_ref[0, local, :, lo].astype(f32) * sine
            v1 = vel_ref[1, local, :, lo].astype(f32)
            w0 = vel_ref[0, local, :, hi].astype(f32) * sine
            w1 = vel_ref[1, local, :, hi].astype(f32)
            s_e = se[rows, lo]
            s_o = so[rows, lo]
            z_e = ze[rows, lo]
            z_o = zo[rows, lo]
            near = v0 * (s_e + s_o) + v1 * (z_e + z_o)
            far = w0 * (s_e - s_o) + w1 * (z_e - z_o)
            ue[rows, lo] = (near + far).astype(bf16)
            uo[rows, lo] = (near - far).astype(bf16)
        return 0

    lax.fori_loop(0, 16, flux, 0)
    for dst, src, first in ((oe, ue, 0), (oo, uo, 512)):
        res = lax.dot_general(src[...], a_ref[first : first + 512, :], NT, preferred_element_type=f32)
        for ta in range(4):
            dst[ta] = res[:, 128 * ta : 128 * ta + 128]
    for ta in range(4):
        for ip in range(8):
            i0 = pl.ds(2 * ip, 16, stride=16)
            i1 = pl.ds(2 * ip + 1, 16, stride=16)
            parts = swap_chunks(oe[ta, i0, :], oo[ta, i0, :], oe[ta, i1, :], oo[ta, i1, :])
            for al in range(4):
                out_ref[4 * ta + al, :, 128 * ip : 128 * ip + 128] = parts[al].astype(bf16)


def grid_stage(recv, velocity, tables, ints, sines):
    whole = pl.BlockSpec((1024, NH), lambda g, *_: (0, 0), pipeline_mode=pl.Buffered(1))

    def latitude_block(g, ints, sines):
        return (0, jnp.where(ints[3] == 1, 2 - g, g), 0, 0)

    wide = [pltpu.VMEM((256, NH), f32)] * 4
    return pl.pallas_call(
        grid_kernel,
        grid_spec=pltpu.PrefetchScalarGridSpec(
            num_scalar_prefetch=2,
            grid=(3,),
            in_specs=[
                pl.BlockSpec((128, 32, 128), lambda g, *_: (0, g, 0)),
                pl.BlockSpec((2, 16, 16, NLON), latitude_block),
                whole,
                whole,
                whole,
            ],
            out_specs=pl.BlockSpec((16, 16, 1024), lambda g, *_: (0, g, 0)),
            scratch_shapes=[pltpu.VMEM((2048, 128), f32)] * 2
            + [pltpu.VMEM((256, 512), bf16)] * 4
            + wide
            + [pltpu.VMEM((256, NH), bf16)] * 2
            + [pltpu.VMEM((4, 256, 128), f32)] * 2,
        ),
        out_shape=jax.ShapeDtypeStruct((16, 48, 1024), bf16),
        compiler_params=params(),
        cost_estimate=pl.CostEstimate(flops=3700000000, bytes_accessed=14000000, transcendentals=0),
        name="grid",
    )(ints, sines, recv, velocity, *tables)


def analyse_body(par_ref, recv_ref, low_ref, up_ref, out_low, out_up, plus, minus, part_p, part_m):
    step = pl.program_id(0)

    @pl.when(step == 0)
    def _():
        for t in range(8):
            lanes = slice(128 * t, 128 * t + 128)
            for a in range(8):
                north = recv_ref[a, :, lanes].astype(f32)
                south = recv_ref[15 - a, :, lanes].astype(f32)
                part_p[48 * a : 48 * a + 48, :] = north + south
                part_m[48 * a : 48 * a + 48, :] = north - south
            for b in range(3):
                rows = slice(128 * b, 128 * b + 128)
                plus[b, lanes, :] = part_p[rows, :].T
                minus[b, lanes, :] = part_m[rows, :].T

    for q in range(2):
        pair = step * 2 + q
        h0 = par_ref[pair]
        for lu in range(2):
            h = h0 if lu == 0 else 1 - h0
            base = h * 32 + pair * 2
            left = jnp.concatenate(
                [
                    jnp.concatenate([ref[b, pl.ds(base + c, 16, stride=64), :] for b in range(3)], 1)
                    for ref in (plus, minus)
                    for c in range(2)
                ],
                0,
            ).astype(bf16)
            table = low_ref[q] if lu == 0 else up_ref[q]
            res = lax.dot_general(left, table, NT, preferred_element_type=f32)
            degree = lax.broadcasted_iota(jnp.int32, (32, res.shape[1]), 1)
            res = jnp.where((degree + h) % 2 == 0, res[0:32], res[32:64]).astype(bf16)
            if lu == 0:
                out_low[q, 0] = res[0:16]
                out_low[q, 1] = res[16:32]
            else:
                zero = jnp.zeros((16, 256), bf16)
                for c in range(2):
                    out_up[q, c, :, 0:256] = zero
                    out_up[q, c, :, 256:512] = res[16 * c : 16 * c + 16]


def analyse(recv, low, up, parity):
    out = pl.BlockSpec((2, 2, 16, LMAX), lambda g, *_: (g, 0, 0, 0))
    return pl.pallas_call(
        analyse_body,
        grid_spec=pltpu.PrefetchScalarGridSpec(
            num_scalar_prefetch=1,
            grid=(8,),
            in_specs=[
                pl.BlockSpec((16, 48, 1024), lambda g, *_: (0, 0, 0), pipeline_mode=pl.Buffered(1)),
                pl.BlockSpec((2, LMAX, HALF), lambda g, *_: (g, 0, 0)),
                pl.BlockSpec((2, LMAX // 2, HALF), lambda g, *_: (g, 0, 0)),
            ],
            out_specs=[out, out],
            scratch_shapes=[
                pltpu.VMEM((3, 1024, 128), f32),
                pltpu.VMEM((3, 1024, 128), f32),
                pltpu.VMEM((HALF, 128), f32),
                pltpu.VMEM((HALF, 128), f32),
            ],
        ),
        out_shape=[jax.ShapeDtypeStruct((16, 2, 16, LMAX), bf16)] * 2,
        compiler_params=params(),
        cost_estimate=pl.CostEstimate(flops=1200000000, bytes_accessed=12000000, transcendentals=0),
        name="analyse",
    )(parity, recv, low, up)


def local(source_coeffs, inverses, velocity, order_slots):
    rad_index = lax.axis_index("rad")
    ang_index = lax.axis_index("ang")
    blocks = order_slots.reshape(16, 2, 16)
    lower = blocks[:, 0]
    upper = blocks[:, 1]
    is_even = lower % 2 == 0
    even = jnp.where(is_even, lower, upper)
    odd = jnp.where(is_even, upper, lower)
    by_source = [v.reshape(16, 8, 2).transpose(1, 0, 2).reshape(256) for v in (even, odd)]
    synth_orders = jnp.concatenate(by_source)
    analyse_orders = jnp.concatenate([even.reshape(256), odd.reshape(256)])
    my_orders = lax.dynamic_slice_in_dim(order_slots, ang_index * 32, 32, 0)
    parity = my_orders[:16] % 2
    south = (ang_index >= 8).astype(jnp.int32)
    ints = jnp.concatenate(
        [rad_index[None].astype(jnp.int32), lax.dynamic_slice_in_dim(parity, rad_index * 2, 2, 0), south[None]]
    )
    position = jnp.arange(48, dtype=jnp.int32)
    latitude = ang_index * 48 + jnp.where(south == 1, 47 - position, position)
    sines = jnp.sin((latitude.astype(f32) + 0.5) * (math.pi / NLAT))

    sent = solve(source_coeffs, inverses, my_orders, rad_index)
    coeffs = lax.all_to_all(sent, "rad", 0, 0, tiled=True)
    low, up = legendre_tables(my_orders)
    tables = fourier_tables(synth_orders, analyse_orders)
    fields = synth(coeffs, low, up, ints)
    fields = lax.all_to_all(fields, ("rad", "ang"), 0, 0, tiled=True)
    fourier = grid_stage(fields, velocity, tables, ints, sines)
    fourier = lax.all_to_all(fourier, "ang", 0, 0, tiled=True)
    out_low, out_up = analyse(fourier, low, up, parity)
    return jnp.concatenate([out_low, out_up], 0)


def solution(mesh):
    in_specs = (P("ang", "rad", None, None), P("rad", None, None), P(None, "ang", "rad", None), P())
    out_specs = P("ang", None, "rad", None)
    return jax.shard_map(local, mesh=mesh, in_specs=in_specs, out_specs=out_specs, check_vma=False)
```

```python
import functools
import math

import jax
import jax.numpy as jnp
import numpy as np
from jax import lax
from jax.experimental import pallas as pl
from jax.experimental.pallas import tpu as pltpu
from jax.sharding import PartitionSpec as P

f32 = jnp.float32
bf16 = jnp.bfloat16
inner_radius = 0.35
grow_bound = 1e10
grow_log = 23.025850929940457
start_log = -1.2051210046670229
vmem_bytes = 60 * 1024 * 1024

LMAX, NLAT, NLON, NR, K = 512, 768, 1536, 128, 128
HALF = NLAT // 2
NH = NLON // 2
NT = (((1,), (1,)), ((), ()))
TN = (((0,), (0,)), ((), ()))


def radial_matrix():
    u = (np.arange(NR) + 0.5) * (math.pi / NR)
    k = np.arange(K)[:, None]
    r = inner_radius + (1.0 - inner_radius) * (np.cos(u) + 1.0) * 0.5
    value = np.cos(k * u[None])
    slope = k * np.sin(k * u[None]) / np.sin(u)[None] * (2.0 / (1.0 - inner_radius))
    both = np.stack([value / r, slope + 3.0 * value / r], 0)
    both = both.reshape(2, K, 8, 16).transpose(1, 2, 0, 3).reshape(K, 256)
    out = np.zeros((2, K, 2, 256))
    out[0, :, 0] = both
    out[1, :, 1] = both
    return jnp.asarray(out.reshape(256, 512), f32).astype(bf16)


def params(sem=("arbitrary",)):
    return pltpu.CompilerParams(dimension_semantics=sem, vmem_limit_bytes=vmem_bytes)


def swap_chunks(x0, x1, x2, x3):
    lane = lax.broadcasted_iota(jnp.int32, x0.shape, 1)
    low = lane < 64
    even = (lane // 32) % 2 == 0
    a0 = jnp.where(low, x0, pltpu.roll(x2, 64, 1))
    a2 = jnp.where(low, pltpu.roll(x0, 64, 1), x2)
    a1 = jnp.where(low, x1, pltpu.roll(x3, 64, 1))
    a3 = jnp.where(low, pltpu.roll(x1, 64, 1), x3)
    y0 = jnp.where(even, a0, pltpu.roll(a1, 32, 1))
    y1 = jnp.where(even, pltpu.roll(a0, 96, 1), a1)
    y2 = jnp.where(even, a2, pltpu.roll(a3, 32, 1))
    y3 = jnp.where(even, pltpu.roll(a2, 96, 1), a3)
    return (y0, y1, y2, y3)


def solve_kernel(base_ref, src_ref, inv_ref, order_ref, out_ref, wide, acc):
    step = pl.program_id(0)
    steps = pl.num_programs(0)
    block = inv_ref.shape[0]

    @pl.when(step == 0)
    def _():
        def widen(s, _):
            wide[pl.ds(pl.multiple_of(s * 128, 128), 128), :] = src_ref[s].astype(f32)
            return 0

        lax.fori_loop(0, 32, widen, 0, unroll=4)

    order = order_ref[...]

    def degree(i, _):
        row = step * block + i
        x0 = wide[pl.ds(2 * row, 32, stride=128), :]
        x1 = wide[pl.ds(2 * row + 1, 32, stride=128), :]
        x = jnp.concatenate([x0, x1], 0).astype(bf16)
        y = lax.dot_general(x, inv_ref[i], NT, preferred_element_type=f32)
        y = jnp.where(order <= base_ref[0] + row, y, 0.0)
        acc[pl.ds(row, 64, stride=64), :] = y
        return 0

    lax.fori_loop(0, block, degree, 0, unroll=8)

    @pl.when(step == steps - 1)
    def _():
        for r in range(8):
            for lu in range(2):
                for q in range(2):
                    for c in range(2):
                        plane = c * 32 + lu * 16 + 2 * r + q
                        row = (lu * 4 + q * 2 + c) * 64
                        out_ref[r, row : row + 64, :] = acc[plane * 64 : plane * 64 + 64, :].astype(bf16)


def solve(source, inverses, orders, rad_index):
    src = source.reshape(32, 128, 128)
    order = jnp.broadcast_to(jnp.tile(orders, 2)[:, None], (64, 128))
    return pl.pallas_call(
        solve_kernel,
        grid_spec=pltpu.PrefetchScalarGridSpec(
            num_scalar_prefetch=1,
            grid=(4,),
            in_specs=[
                pl.BlockSpec((32, 128, 128), lambda g, b: (0, 0, 0)),
                pl.BlockSpec((16, 128, 128), lambda g, b: (g, 0, 0)),
                pl.BlockSpec((64, 128), lambda g, b: (0, 0)),
            ],
            out_specs=pl.BlockSpec((8, 512, 128), lambda g, b: (0, 0, 0)),
            scratch_shapes=[pltpu.VMEM((4096, 128), f32), pltpu.VMEM((4096, 128), f32)],
        ),
        out_shape=jax.ShapeDtypeStruct((8, 512, 128), bf16),
        compiler_params=params(),
        cost_estimate=pl.CostEstimate(flops=134217728, bytes_accessed=4194304, transcendentals=0),
        name="solve",
    )(jnp.reshape(rad_index * 64, (1,)), src, inverses, order)


def legendre_kernel(groups, c1_ref, c2_ref, m_ref, x_ref, log_ref, *refs):
    outs = refs[: len(groups)]
    p1, p2, lg, bp, tile = refs[len(groups) :]
    step = pl.program_id(0)

    @pl.when(step == 0)
    def _():
        p1[...] = jnp.zeros(p1.shape, f32)
        p2[...] = jnp.zeros(p2.shape, f32)
        bp[...] = jnp.zeros(bp.shape, f32)
        lg[...] = log_ref[...]

    def run(start, count, out_ref):
        rows = slice(start, start + count)
        m = m_ref[rows, :]
        m2 = m * m
        lanes = [slice(128 * t, 128 * t + 128) for t in range(3)]

        def sub(b, state):
            cur, prev, logs, below = state
            scale = [jnp.exp(v) for v in logs]
            for i in range(8):
                local = b * 8 + i
                l = step * 32 + local
                lf = l.astype(f32)
                d = jnp.maximum(lf * lf - m2, 1.0)
                r = lax.rsqrt(d)
                r = r * (1.5 - 0.5 * d * r * r)
                a = c1_ref[l] * r
                ab = a * below
                below = d * r * c2_ref[l]
                seed = jnp.where(m == lf, 1.0, 0.0)
                for t in range(3):
                    new = (a * x_ref[0:count, lanes[t]]) * cur[t] - ab * prev[t] + seed
                    prev[t] = cur[t]
                    cur[t] = new
                    tile[t, pl.ds(local, count, stride=32), :] = new * scale[t]
            for t in range(3):
                big = jnp.abs(cur[t]) > grow_bound
                factor = jnp.where(big, 1.0 / grow_bound, 1.0)
                cur[t] = cur[t] * factor
                prev[t] = prev[t] * factor
                logs[t] = logs[t] + jnp.where(big, grow_log, 0.0)
            return (cur, prev, logs, below)

        state = (
            [p1[rows, v] for v in lanes],
            [p2[rows, v] for v in lanes],
            [lg[rows, v] for v in lanes],
            bp[rows, :],
        )
        cur, prev, logs, below = lax.fori_loop(0, 4, sub, state)
        for t in range(3):
            p1[rows, lanes[t]] = cur[t]
            p2[rows, lanes[t]] = prev[t]
            lg[rows, lanes[t]] = logs[t]
        bp[rows, :] = below
        for s in range(out_ref.shape[0]):
            for t in range(3):
                out_ref[s, :, lanes[t]] = tile[t, s * 32 : s * 32 + 32, :].astype(bf16)

    for (start, count, _, first), out_ref in zip(groups, outs):
        if first == 0:
            run(start, count, out_ref)
        else:
            pl.when(step >= first)(lambda: run(start, count, out_ref))


def legendre_tables(orders, groups, name):
    total = orders.shape[0]
    l = np.arange(LMAX, dtype=np.float64)
    root = np.sqrt(np.maximum(4.0 * l * l - 1.0, 1.0))
    t = (np.arange(HALF) + 0.5) * (math.pi / NLAT)
    gammas = [0.5 * (math.lgamma(m + 1.5) - math.lgamma(m + 1.0)) + start_log for m in range(LMAX)]
    x = jnp.asarray(np.broadcast_to(np.cos(t), (16, HALF)), f32)
    mf = orders.astype(f32)
    logs = jnp.take(jnp.asarray(gammas, f32), orders)[:, None] + mf[:, None] * jnp.asarray(np.log(np.sin(t)), f32)[None]

    def out_spec(slots, first):
        return pl.BlockSpec((slots, 32, HALF), lambda g, *_: (0, jnp.maximum(g - first, 0), 0))

    return pl.pallas_call(
        functools.partial(legendre_kernel, groups),
        grid_spec=pltpu.PrefetchScalarGridSpec(
            num_scalar_prefetch=2,
            grid=(16,),
            in_specs=[
                pl.BlockSpec((total, 128), lambda g, *_: (0, 0)),
                pl.BlockSpec((16, HALF), lambda g, *_: (0, 0)),
                pl.BlockSpec((total, HALF), lambda g, *_: (0, 0)),
            ],
            out_specs=[out_spec(slots, first) for _, _, slots, first in groups],
            scratch_shapes=[
                pltpu.VMEM((total, HALF), f32),
                pltpu.VMEM((total, HALF), f32),
                pltpu.VMEM((total, HALF), f32),
                pltpu.VMEM((total, 128), f32),
                pltpu.VMEM((3, 512, 128), f32),
            ],
        ),
        out_shape=[jax.ShapeDtypeStruct((slots, LMAX - 32 * first, HALF), bf16) for _, _, slots, first in groups],
        compiler_params=params(),
        cost_estimate=pl.CostEstimate(flops=2000000 * total, bytes_accessed=400000 * total, transcendentals=3000 * total),
        name=name,
    )(
        jnp.asarray(root, f32),
        jnp.asarray(1.0 / root, f32),
        jnp.broadcast_to(mf[:, None], (total, 128)),
        x,
        logs,
    )


def phase_rows(orders):
    m = jnp.repeat(orders, 2)[:, None]
    c = jnp.tile(jnp.asarray([0, NLON // 4], jnp.int32), orders.shape[0])[:, None]
    near = (m * jnp.arange(128, dtype=jnp.int32)[None] + c) % NLON
    far = (m * (128 * jnp.arange(8, dtype=jnp.int32))[None]) % NLON
    near = near.astype(f32) * (2.0 * math.pi / NLON)
    far = far.astype(f32) * (2.0 * math.pi / NLON)
    return (jnp.cos(near), jnp.sin(near), jnp.cos(far), jnp.sin(far))


def table_kernel(nc, ns, fc, fs, w, t_ref, d_ref, a_ref):
    scale = (2.0 * math.pi / NLON) * (math.pi / NLAT)
    weight = w[:, 0:1]
    turn = w[:, 1:2]
    for b in range(6):
        lanes = slice(128 * b, 128 * b + 128)
        cosine = fc[:, b : b + 1] * nc[...] - fs[:, b : b + 1] * ns[...]
        sine = fs[:, b : b + 1] * nc[...] + fc[:, b : b + 1] * ns[...]
        t_ref[:, lanes] = (weight * cosine).astype(bf16)
        d_ref[:, lanes] = (turn * sine).astype(bf16)
        a_ref[:, lanes] = (scale * cosine).astype(bf16)


def fourier_tables(rows, orders):
    m = jnp.repeat(orders, 2).astype(f32)
    w = jnp.where(m == 0.0, 1.0, 2.0)
    weights = jnp.stack([w, -m * w] * 4, 1)
    near = pl.BlockSpec((256, 128), lambda g: (g, 0))
    far = pl.BlockSpec((256, 8), lambda g: (g, 0))
    out = pl.BlockSpec((256, NH), lambda g: (g, 0))
    return pl.pallas_call(
        table_kernel,
        grid=(4,),
        in_specs=[near, near, far, far, far],
        out_specs=[out, out, out],
        out_shape=[jax.ShapeDtypeStruct((1024, NH), bf16)] * 3,
        compiler_params=params(),
        cost_estimate=pl.CostEstimate(flops=8000000, bytes_accessed=8000000, transcendentals=0),
        name="tables",
    )(*rows, weights)


def synth_kernel(ints_ref, recv_ref, leg_ref, mat_ref, out_ref, ns, scr):
    mat = mat_ref[...]
    for lu in range(2):
        for q in range(2):
            first = 4 * lu
            count = 64 * (8 - first)
            h = ints_ref[1 + q]
            h = h if lu == 0 else 1 - h
            planes = []
            for c in range(2):
                row = (lu * 4 + q * 2 + c) * 64
                planes.append(recv_ref[first:8, row : row + 64, :].reshape(count, 128))
            coeffs = jnp.concatenate(planes, 1)
            rad = jnp.dot(coeffs, mat, preferred_element_type=f32)
            degree = lax.broadcasted_iota(jnp.int32, rad.shape, 0)
            sign = (1 - 2 * ((degree + h) % 2)).astype(f32)
            both = jnp.concatenate([rad.astype(bf16), (rad * sign).astype(bf16)], 1)
            table = leg_ref[lu * 2 + q, 64 * first : LMAX, :]
            wave = lax.dot_general(table, both, TN, preferred_element_type=f32)
            for tile in range(8):
                ns[tile] = wave[:, 128 * tile : 128 * tile + 128]
            for half in range(2):
                for c in range(2):
                    for rh in range(2):
                        tile = half * 4 + c * 2 + rh
                        parts = swap_chunks(*[ns[tile, pl.ds(j, 96, stride=4), :] for j in range(4)])
                        for rl in range(4):
                            base = (((rh * 4 + rl) * 2 + half) * 96) * 8 + q * 2 + c
                            scr[pl.ds(base + h * 4, 96, stride=8), :] = parts[rl]

    def emit(i, _):
        r = i % 8
        a = i // 8
        half = a // 8
        north = jnp.where(half == 0, a, 15 - a)
        start = pl.multiple_of(((r * 2 + half) * 96 + north * 12) * 8, 32)
        out_ref[i] = scr[pl.ds(start, 96), :].astype(bf16)
        return 0

    lax.fori_loop(0, 128, emit, 0, unroll=2)


def synth(recv, table, ints):
    return pl.pallas_call(
        synth_kernel,
        grid_spec=pltpu.PrefetchScalarGridSpec(
            num_scalar_prefetch=1,
            grid=(1,),
            in_specs=[
                pl.BlockSpec((8, 512, 128), lambda g, b: (0, 0, 0)),
                pl.BlockSpec((4, LMAX, HALF), lambda g, b: (0, 0, 0)),
                pl.BlockSpec((256, 512), lambda g, b: (0, 0)),
            ],
            out_specs=pl.BlockSpec((128, 96, 128), lambda g, b: (0, 0, 0)),
            scratch_shapes=[pltpu.VMEM((8, HALF, 128), f32), pltpu.VMEM((8 * 2 * 96 * 8, 128), f32)],
        ),
        out_shape=jax.ShapeDtypeStruct((128, 96, 128), bf16),
        compiler_params=params(),
        cost_estimate=pl.CostEstimate(flops=2000000000, bytes_accessed=7000000, transcendentals=0),
        name="synth",
    )(ints, recv, table, radial_matrix())


def grid_kernel(
    ints_ref, sines_ref, recv_ref, vel_ref, t_ref, d_ref, a_ref, out_ref,
    ke, ko, l0e, l0o, l1e, l1o, se, so, ze, zo, ue, uo, oe, oo,
):
    step = pl.program_id(0)
    top = lax.broadcasted_iota(jnp.int32, (8, 128), 0) < 4

    def gather(u, _):
        a = recv_ref[2 * u].astype(f32)
        b = recv_ref[2 * u + 1].astype(f32)
        for t in range(4):
            at = a[8 * t : 8 * t + 8]
            bt = b[8 * t : 8 * t + 8]
            row = pl.multiple_of(t * 512 + 8 * u, 8)
            ke[pl.ds(row, 8), :] = jnp.where(top, at, pltpu.roll(bt, 4, 0))
            ko[pl.ds(row, 8), :] = jnp.where(top, pltpu.roll(at, 4, 0), bt)
        return 0

    lax.fori_loop(0, 64, gather, 0, unroll=4)
    for t in range(4):
        for src, zero, one in ((ke, l0e, l1e), (ko, l0o, l1o)):
            turned = src[512 * t : 512 * t + 512, :].T.astype(bf16)
            for j in range(4):
                row = (t * 4 + j) * 16
                zero[row : row + 16, :] = turned[32 * j : 32 * j + 16]
                one[row : row + 16, :] = turned[32 * j + 16 : 32 * j + 32]
    se[...] = jnp.dot(l1e[...], t_ref[0:512, :], preferred_element_type=f32)
    so[...] = jnp.dot(l1o[...], t_ref[512:1024, :], preferred_element_type=f32)
    ze[...] = jnp.dot(l0e[...], d_ref[0:512, :], preferred_element_type=f32)
    zo[...] = jnp.dot(l0o[...], d_ref[512:1024, :], preferred_element_type=f32)
    south = ints_ref[3]

    def flux(j, _):
        local = jnp.where(south == 1, 15 - j, j)
        sine = sines_ref[step * 16 + j]
        rows = pl.ds(pl.multiple_of(j * 16, 16), 16)
        for b in range(3):
            lo = slice(256 * b, 256 * b + 256)
            hi = slice(NH + 256 * b, NH + 256 * b + 256)
            v0 = vel_ref[0, local, :, lo].astype(f32) * sine
            v1 = vel_ref[1, local, :, lo].astype(f32)
            w0 = vel_ref[0, local, :, hi].astype(f32) * sine
            w1 = vel_ref[1, local, :, hi].astype(f32)
            s_e = se[rows, lo]
            s_o = so[rows, lo]
            z_e = ze[rows, lo]
            z_o = zo[rows, lo]
            near = v0 * (s_e + s_o) + v1 * (z_e + z_o)
            far = w0 * (s_e - s_o) + w1 * (z_e - z_o)
            ue[rows, lo] = (near + far).astype(bf16)
            uo[rows, lo] = (near - far).astype(bf16)
        return 0

    lax.fori_loop(0, 16, flux, 0)
    for dst, src, first in ((oe, ue, 0), (oo, uo, 512)):
        res = lax.dot_general(src[...], a_ref[first : first + 512, :], NT, preferred_element_type=f32)
        for ta in range(4):
            dst[ta] = res[:, 128 * ta : 128 * ta + 128]
    for ta in range(4):
        for ip in range(8):
            i0 = pl.ds(2 * ip, 16, stride=16)
            i1 = pl.ds(2 * ip + 1, 16, stride=16)
            parts = swap_chunks(oe[ta, i0, :], oo[ta, i0, :], oe[ta, i1, :], oo[ta, i1, :])
            for al in range(4):
                out_ref[4 * ta + al, :, 128 * ip : 128 * ip + 128] = parts[al].astype(bf16)


def grid_stage(recv, velocity, tables, ints, sines):
    whole = pl.BlockSpec((1024, NH), lambda g, *_: (0, 0), pipeline_mode=pl.Buffered(1))

    def latitude_block(g, ints, sines):
        return (0, jnp.where(ints[3] == 1, 2 - g, g), 0, 0)

    wide = [pltpu.VMEM((256, NH), f32)] * 4
    return pl.pallas_call(
        grid_kernel,
        grid_spec=pltpu.PrefetchScalarGridSpec(
            num_scalar_prefetch=2,
            grid=(3,),
            in_specs=[
                pl.BlockSpec((128, 32, 128), lambda g, *_: (0, g, 0)),
                pl.BlockSpec((2, 16, 16, NLON), latitude_block),
                whole,
                whole,
                whole,
            ],
            out_specs=pl.BlockSpec((16, 16, 1024), lambda g, *_: (0, g, 0)),
            scratch_shapes=[pltpu.VMEM((2048, 128), f32)] * 2
            + [pltpu.VMEM((256, 512), bf16)] * 4
            + wide
            + [pltpu.VMEM((256, NH), bf16)] * 2
            + [pltpu.VMEM((4, 256, 128), f32)] * 2,
        ),
        out_shape=jax.ShapeDtypeStruct((16, 48, 1024), bf16),
        compiler_params=params(),
        cost_estimate=pl.CostEstimate(flops=3700000000, bytes_accessed=14000000, transcendentals=0),
        name="grid",
    )(ints, sines, recv, velocity, *tables)


def analyse_body(par_ref, recv_ref, low_ref, up_ref, out_ref, plus, minus, part_p, part_m):
    step = pl.program_id(0)

    @pl.when(step == 0)
    def _():
        for t in range(8):
            lanes = slice(128 * t, 128 * t + 128)
            for a in range(8):
                north = recv_ref[a, :, lanes].astype(f32)
                south = recv_ref[15 - a, :, lanes].astype(f32)
                part_p[48 * a : 48 * a + 48, :] = north + south
                part_m[48 * a : 48 * a + 48, :] = north - south
            for b in range(3):
                rows = slice(128 * b, 128 * b + 128)
                plus[b, lanes, :] = part_p[rows, :].T
                minus[b, lanes, :] = part_m[rows, :].T

    for q in range(2):
        pair = step * 2 + q
        h0 = par_ref[pair]
        for lu in range(2):
            h = h0 if lu == 0 else 1 - h0
            base = h * 32 + pair * 2
            left = jnp.concatenate(
                [
                    jnp.concatenate([ref[b, pl.ds(base + c, 16, stride=64), :] for b in range(3)], 1)
                    for ref in (plus, minus)
                    for c in range(2)
                ],
                0,
            ).astype(bf16)
            table = low_ref[q] if lu == 0 else up_ref[q]
            res = lax.dot_general(left, table, NT, preferred_element_type=f32)
            degree = lax.broadcasted_iota(jnp.int32, (32, res.shape[1]), 1)
            res = jnp.where((degree + h) % 2 == 0, res[0:32], res[32:64]).astype(bf16)
            if lu == 0:
                out_ref[0, q, 0] = res[0:16]
                out_ref[0, q, 1] = res[16:32]
            else:
                zero = jnp.zeros((16, 256), bf16)
                for c in range(2):
                    out_ref[1, q, c, :, 0:256] = zero
                    out_ref[1, q, c, :, 256:512] = res[16 * c : 16 * c + 16]


def analyse(recv, low, up, parity):
    out = pl.BlockSpec((2, 2, 2, 16, LMAX), lambda g, *_: (0, g, 0, 0, 0))
    return pl.pallas_call(
        analyse_body,
        grid_spec=pltpu.PrefetchScalarGridSpec(
            num_scalar_prefetch=1,
            grid=(8,),
            in_specs=[
                pl.BlockSpec((16, 48, 1024), lambda g, *_: (0, 0, 0), pipeline_mode=pl.Buffered(1)),
                pl.BlockSpec((2, LMAX, HALF), lambda g, *_: (g, 0, 0)),
                pl.BlockSpec((2, LMAX // 2, HALF), lambda g, *_: (g, 0, 0)),
            ],
            out_specs=out,
            scratch_shapes=[
                pltpu.VMEM((3, 1024, 128), f32),
                pltpu.VMEM((3, 1024, 128), f32),
                pltpu.VMEM((HALF, 128), f32),
                pltpu.VMEM((HALF, 128), f32),
            ],
        ),
        out_shape=jax.ShapeDtypeStruct((2, 16, 2, 16, LMAX), bf16),
        compiler_params=params(),
        cost_estimate=pl.CostEstimate(flops=1200000000, bytes_accessed=12000000, transcendentals=0),
        name="analyse",
    )(parity, recv, low, up)


def local(source_coeffs, inverses, velocity, order_slots):
    rad_index = lax.axis_index("rad")
    ang_index = lax.axis_index("ang")
    blocks = order_slots.reshape(16, 2, 16)
    lower = blocks[:, 0]
    upper = blocks[:, 1]
    is_even = lower % 2 == 0
    even = jnp.where(is_even, lower, upper)
    odd = jnp.where(is_even, upper, lower)
    fourier_orders = jnp.concatenate([even.reshape(256), odd.reshape(256)])
    my_orders = lax.dynamic_slice_in_dim(order_slots, ang_index * 32, 32, 0)
    parity = my_orders[:16] % 2
    south = (ang_index >= 8).astype(jnp.int32)
    ints = jnp.concatenate(
        [rad_index[None].astype(jnp.int32), lax.dynamic_slice_in_dim(parity, rad_index * 2, 2, 0), south[None]]
    )
    position = jnp.arange(48, dtype=jnp.int32)
    latitude = ang_index * 48 + jnp.where(south == 1, 47 - position, position)
    sines = jnp.sin((latitude.astype(f32) + 0.5) * (math.pi / NLAT))

    sent = solve(source_coeffs, inverses, my_orders, rad_index)
    early, sent = lax.optimization_barrier((fourier_orders, sent))
    coeffs = lax.all_to_all(sent, "rad", 0, 0, tiled=True)
    pairs = [lax.dynamic_slice_in_dim(v, rad_index * 2, 2, 0) for v in (my_orders[:16], my_orders[16:])]
    own_orders = jnp.concatenate(pairs * 2)
    (own,) = legendre_tables(own_orders, ((0, 8, 4, 0),), "legendre_own")
    rows = phase_rows(early)
    coeffs, own, rows = lax.optimization_barrier((coeffs, own, rows))
    fields = synth(coeffs, own, ints)
    fields, late, rows = lax.optimization_barrier((fields, my_orders, rows))
    fields = lax.all_to_all(fields, ("ang", "rad"), 0, 0, tiled=True)
    low, up = legendre_tables(late, ((0, 16, 16, 0), (16, 16, 16, 8)), "legendre")
    tables = fourier_tables(rows, fourier_orders)
    fields, low, up, tables = lax.optimization_barrier((fields, low, up, tables))
    fourier = grid_stage(fields, velocity, tables, ints, sines)
    fourier = lax.all_to_all(fourier, "ang", 0, 0, tiled=True)
    return analyse(fourier, low, up, parity).reshape(32, 2, 16, LMAX)


def solution(mesh):
    in_specs = (P("ang", "rad", None, None), P("rad", None, None), P(None, "ang", "rad", None), P())
    out_specs = P("ang", None, "rad", None)
    return jax.shard_map(local, mesh=mesh, in_specs=in_specs, out_specs=out_specs, check_vma=False)
```

```python
import functools
import math

import jax
import jax.numpy as jnp
import numpy as np
from jax import lax
from jax.experimental import pallas as pl
from jax.experimental.pallas import tpu as pltpu
from jax.sharding import PartitionSpec as P

f32 = jnp.float32
bf16 = jnp.bfloat16
inner_radius = 0.35
grow_bound = 1e10
grow_log = 23.025850929940457
start_log = -1.2051210046670229
vmem_bytes = 60 * 1024 * 1024

LMAX, NLAT, NLON, NR, K = 512, 768, 1536, 128, 128
HALF = NLAT // 2
NH = NLON // 2
NT = (((1,), (1,)), ((), ()))
TN = (((0,), (0,)), ((), ()))


def radial_matrix():
    u = (np.arange(NR) + 0.5) * (math.pi / NR)
    k = np.arange(K)[:, None]
    r = inner_radius + (1.0 - inner_radius) * (np.cos(u) + 1.0) * 0.5
    value = np.cos(k * u[None])
    slope = k * np.sin(k * u[None]) / np.sin(u)[None] * (2.0 / (1.0 - inner_radius))
    both = np.stack([value / r, slope + 3.0 * value / r], 0)
    both = both.reshape(2, K, 8, 16).transpose(1, 2, 0, 3).reshape(K, 8, 32)
    out = np.zeros((2, K, 8, 2, 32))
    out[0, :, :, 0] = both
    out[1, :, :, 1] = both
    return jnp.asarray(out.reshape(256, 512), f32).astype(bf16)


def params(sem=("arbitrary",)):
    return pltpu.CompilerParams(dimension_semantics=sem, vmem_limit_bytes=vmem_bytes)


def swap_chunks(x0, x1, x2, x3):
    lane = lax.broadcasted_iota(jnp.int32, x0.shape, 1)
    low = lane < 64
    even = (lane // 32) % 2 == 0
    a0 = jnp.where(low, x0, pltpu.roll(x2, 64, 1))
    a2 = jnp.where(low, pltpu.roll(x0, 64, 1), x2)
    a1 = jnp.where(low, x1, pltpu.roll(x3, 64, 1))
    a3 = jnp.where(low, pltpu.roll(x1, 64, 1), x3)
    y0 = jnp.where(even, a0, pltpu.roll(a1, 32, 1))
    y1 = jnp.where(even, pltpu.roll(a0, 96, 1), a1)
    y2 = jnp.where(even, a2, pltpu.roll(a3, 32, 1))
    y3 = jnp.where(even, pltpu.roll(a2, 96, 1), a3)
    return (y0, y1, y2, y3)


def solve_kernel(base_ref, src_ref, inv_ref, order_ref, out_ref, wide, acc):
    step = pl.program_id(0)
    steps = pl.num_programs(0)
    block = inv_ref.shape[0]

    @pl.when(step == 0)
    def _():
        def widen(s, _):
            wide[pl.ds(pl.multiple_of(s * 136, 8), 128), :] = src_ref[s].astype(f32)
            return 0

        lax.fori_loop(0, 32, widen, 0, unroll=4)

    order = order_ref[...]

    def degree(i, _):
        row = step * block + i
        x0 = wide[pl.ds(2 * row, 32, stride=136), :]
        x1 = wide[pl.ds(2 * row + 1, 32, stride=136), :]
        x = jnp.concatenate([x0, x1], 0).astype(bf16)
        y = lax.dot_general(x, inv_ref[i], NT, preferred_element_type=f32)
        y = jnp.where(order <= base_ref[0] + row, y, 0.0)
        acc[pl.ds(row, 64, stride=72), :] = y
        return 0

    lax.fori_loop(0, block, degree, 0, unroll=8)

    @pl.when(step == steps - 1)
    def _():
        for r in range(8):
            for lu in range(2):
                for q in range(2):
                    for c in range(2):
                        plane = c * 32 + lu * 16 + 2 * r + q
                        row = (lu * 4 + q * 2 + c) * 64
                        out_ref[r, row : row + 64, :] = acc[plane * 72 : plane * 72 + 64, :].astype(bf16)


def solve(source, inverses, orders, rad_index):
    src = source.reshape(32, 128, 128)
    order = jnp.broadcast_to(jnp.tile(orders, 2)[:, None], (64, 128))
    return pl.pallas_call(
        solve_kernel,
        grid_spec=pltpu.PrefetchScalarGridSpec(
            num_scalar_prefetch=1,
            grid=(4,),
            in_specs=[
                pl.BlockSpec((32, 128, 128), lambda g, b: (0, 0, 0)),
                pl.BlockSpec((16, 128, 128), lambda g, b: (g, 0, 0)),
                pl.BlockSpec((64, 128), lambda g, b: (0, 0)),
            ],
            out_specs=pl.BlockSpec((8, 512, 128), lambda g, b: (0, 0, 0)),
            scratch_shapes=[pltpu.VMEM((32 * 136, 128), f32), pltpu.VMEM((64 * 72, 128), f32)],
        ),
        out_shape=jax.ShapeDtypeStruct((8, 512, 128), bf16),
        compiler_params=params(),
        cost_estimate=pl.CostEstimate(flops=134217728, bytes_accessed=4194304, transcendentals=0),
        name="solve",
    )(jnp.reshape(rad_index * 64, (1,)), src, inverses, order)


def legendre_kernel(groups, c1_ref, c2_ref, m_ref, x_ref, log_ref, *refs):
    outs = refs[: len(groups)]
    p1, p2, lg, bp, tile = refs[len(groups) :]
    step = pl.program_id(0)

    @pl.when(step == 0)
    def _():
        p1[...] = jnp.zeros(p1.shape, f32)
        p2[...] = jnp.zeros(p2.shape, f32)
        bp[...] = jnp.zeros(bp.shape, f32)
        lg[...] = log_ref[...]

    def run(start, count, out_ref):
        rows = slice(start, start + count)
        m = m_ref[rows, :]
        m2 = m * m
        lanes = [slice(128 * t, 128 * t + 128) for t in range(3)]

        def sub(b, state):
            cur, prev, logs, below = state
            scale = [jnp.exp(v) for v in logs]
            for i in range(8):
                local = b * 8 + i
                l = step * 32 + local
                lf = l.astype(f32)
                d = jnp.maximum(lf * lf - m2, 1.0)
                r = lax.rsqrt(d)
                r = r * (1.5 - 0.5 * d * r * r)
                a = c1_ref[l] * r
                ab = a * below
                below = d * r * c2_ref[l]
                seed = jnp.where(m == lf, 1.0, 0.0)
                for t in range(3):
                    new = (a * x_ref[0:count, lanes[t]]) * cur[t] - ab * prev[t] + seed
                    prev[t] = cur[t]
                    cur[t] = new
                    tile[t, pl.ds(local, count, stride=40), :] = new * scale[t]
            for t in range(3):
                big = jnp.abs(cur[t]) > grow_bound
                factor = jnp.where(big, 1.0 / grow_bound, 1.0)
                cur[t] = cur[t] * factor
                prev[t] = prev[t] * factor
                logs[t] = logs[t] + jnp.where(big, grow_log, 0.0)
            return (cur, prev, logs, below)

        state = (
            [p1[rows, v] for v in lanes],
            [p2[rows, v] for v in lanes],
            [lg[rows, v] for v in lanes],
            bp[rows, :],
        )
        cur, prev, logs, below = lax.fori_loop(0, 4, sub, state)
        for t in range(3):
            p1[rows, lanes[t]] = cur[t]
            p2[rows, lanes[t]] = prev[t]
            lg[rows, lanes[t]] = logs[t]
        bp[rows, :] = below
        for s in range(out_ref.shape[0]):
            for t in range(3):
                out_ref[s, :, lanes[t]] = tile[t, s * 40 : s * 40 + 32, :].astype(bf16)

    for (start, count, _, first), out_ref in zip(groups, outs):
        if first == 0:
            run(start, count, out_ref)
        else:
            pl.when(step >= first)(lambda: run(start, count, out_ref))


def legendre_tables(orders, groups, name):
    total = orders.shape[0]
    l = np.arange(LMAX, dtype=np.float64)
    root = np.sqrt(np.maximum(4.0 * l * l - 1.0, 1.0))
    t = (np.arange(HALF) + 0.5) * (math.pi / NLAT)
    gammas = [0.5 * (math.lgamma(m + 1.5) - math.lgamma(m + 1.0)) + start_log for m in range(LMAX)]
    x = jnp.asarray(np.broadcast_to(np.cos(t), (16, HALF)), f32)
    mf = orders.astype(f32)
    logs = jnp.take(jnp.asarray(gammas, f32), orders)[:, None] + mf[:, None] * jnp.asarray(np.log(np.sin(t)), f32)[None]

    def out_spec(slots, first):
        return pl.BlockSpec((slots, 32, HALF), lambda g, *_: (0, jnp.maximum(g - first, 0), 0))

    return pl.pallas_call(
        functools.partial(legendre_kernel, groups),
        grid_spec=pltpu.PrefetchScalarGridSpec(
            num_scalar_prefetch=2,
            grid=(16,),
            in_specs=[
                pl.BlockSpec((total, 128), lambda g, *_: (0, 0)),
                pl.BlockSpec((16, HALF), lambda g, *_: (0, 0)),
                pl.BlockSpec((total, HALF), lambda g, *_: (0, 0)),
            ],
            out_specs=[out_spec(slots, first) for _, _, slots, first in groups],
            scratch_shapes=[
                pltpu.VMEM((total, HALF), f32),
                pltpu.VMEM((total, HALF), f32),
                pltpu.VMEM((total, HALF), f32),
                pltpu.VMEM((total, 128), f32),
                pltpu.VMEM((3, 640, 128), f32),
            ],
        ),
        out_shape=[jax.ShapeDtypeStruct((slots, LMAX - 32 * first, HALF), bf16) for _, _, slots, first in groups],
        compiler_params=params(),
        cost_estimate=pl.CostEstimate(flops=2000000 * total, bytes_accessed=400000 * total, transcendentals=3000 * total),
        name=name,
    )(
        jnp.asarray(root, f32),
        jnp.asarray(1.0 / root, f32),
        jnp.broadcast_to(mf[:, None], (total, 128)),
        x,
        logs,
    )


def phase_rows(orders):
    m = orders[:, None]
    near = (m * jnp.arange(128, dtype=jnp.int32)[None]) % NLON
    far = (m * (128 * jnp.arange(8, dtype=jnp.int32))[None]) % NLON
    near = near.astype(f32) * (2.0 * math.pi / NLON)
    far = far.astype(f32) * (2.0 * math.pi / NLON)
    m = orders.astype(f32)
    w = jnp.where(m == 0.0, 1.0, 2.0)
    weights = jnp.stack([w, -m * w] * 4, 1)
    return (jnp.cos(near), jnp.sin(near), jnp.cos(far), jnp.sin(far), weights)


def table_kernel(nc, ns, fc, fs, w, t_ref, d_ref, a_ref):
    scale = (2.0 * math.pi / NLON) * (math.pi / NLAT)
    for b in range(6):
        lanes = slice(128 * b, 128 * b + 128)
        parts = []
        for q in range(2):
            rows = slice(128 * q, 128 * q + 128)
            far_cos = fc[rows, b : b + 1]
            far_sin = fs[rows, b : b + 1]
            cosine = far_cos * nc[rows, :] - far_sin * ns[rows, :]
            sine = far_sin * nc[rows, :] + far_cos * ns[rows, :]
            weight = w[rows, 0:1]
            turn = w[rows, 1:2]
            first = slice(256 * q, 256 * q + 128)
            second = slice(256 * q + 128, 256 * q + 256)
            t_ref[first, lanes] = (weight * cosine).astype(bf16)
            t_ref[second, lanes] = (-weight * sine).astype(bf16)
            d_ref[first, lanes] = (turn * sine).astype(bf16)
            d_ref[second, lanes] = (turn * cosine).astype(bf16)
            parts += [scale * cosine, -scale * sine]
        for a in range(16):
            rows = jnp.concatenate([v[8 * a : 8 * a + 8] for v in parts], 0)
            a_ref[32 * a : 32 * a + 32, lanes] = rows.astype(bf16)


def fourier_tables(rows):
    near = pl.BlockSpec((256, 128), lambda g: (g, 0))
    far = pl.BlockSpec((256, 8), lambda g: (g, 0))
    out = pl.BlockSpec((512, NH), lambda g: (g, 0))
    return pl.pallas_call(
        table_kernel,
        grid=(2,),
        in_specs=[near, near, far, far, far],
        out_specs=[out, out, out],
        out_shape=[jax.ShapeDtypeStruct((1024, NH), bf16)] * 3,
        compiler_params=params(),
        cost_estimate=pl.CostEstimate(flops=8000000, bytes_accessed=8000000, transcendentals=0),
        name="tables",
    )(*rows)


def synth_kernel(ints_ref, recv_ref, leg_ref, mat_ref, out_ref, ns):
    mat = mat_ref[...]
    for lu in range(2):
        for q in range(2):
            first = 4 * lu
            count = 64 * (8 - first)
            h = ints_ref[1 + q]
            h = h if lu == 0 else 1 - h
            planes = []
            for c in range(2):
                row = (lu * 4 + q * 2 + c) * 64
                planes.append(recv_ref[first:8, row : row + 64, :].reshape(count, 128))
            coeffs = jnp.concatenate(planes, 1)
            rad = jnp.dot(coeffs, mat, preferred_element_type=f32)
            degree = lax.broadcasted_iota(jnp.int32, rad.shape, 0)
            sign = (1 - 2 * ((degree + h) % 2)).astype(f32)
            both = jnp.concatenate([rad.astype(bf16), (rad * sign).astype(bf16)], 1)
            table = leg_ref[lu * 2 + q, 64 * first : LMAX, :]
            wave = lax.dot_general(table, both, TN, preferred_element_type=f32)
            for tile in range(8):
                ns[lu * 2 + q, tile] = wave[:, 128 * tile : 128 * tile + 128]
    low = lax.broadcasted_iota(jnp.int32, (HALF, 128), 1) < 64
    for h in range(2):
        first, second = [(ints_ref[1 + q] if h == 0 else 1 - ints_ref[1 + q]) * 2 + q for q in range(2)]
        for half in range(2):
            for rh in range(4):
                v0 = ns[first, half * 4 + rh]
                v1 = ns[second, half * 4 + rh]
                parts = (
                    jnp.where(low, v0, pltpu.roll(v1, 64, 1)),
                    jnp.where(low, pltpu.roll(v0, 64, 1), v1),
                )
                for rl in range(2):
                    for north in range(8):
                        a = north if half == 0 else 15 - north
                        rows = parts[rl][48 * north : 48 * north + 48]
                        out_ref[a * 8 + rh * 2 + rl, 48 * h : 48 * h + 48, :] = rows.astype(bf16)


def synth(recv, table, ints):
    return pl.pallas_call(
        synth_kernel,
        grid_spec=pltpu.PrefetchScalarGridSpec(
            num_scalar_prefetch=1,
            grid=(1,),
            in_specs=[
                pl.BlockSpec((8, 512, 128), lambda g, b: (0, 0, 0)),
                pl.BlockSpec((4, LMAX, HALF), lambda g, b: (0, 0, 0)),
                pl.BlockSpec((256, 512), lambda g, b: (0, 0)),
            ],
            out_specs=pl.BlockSpec((128, 96, 128), lambda g, b: (0, 0, 0)),
            scratch_shapes=[pltpu.VMEM((4, 8, HALF, 128), f32)],
        ),
        out_shape=jax.ShapeDtypeStruct((128, 96, 128), bf16),
        compiler_params=params(),
        cost_estimate=pl.CostEstimate(flops=2000000000, bytes_accessed=7000000, transcendentals=0),
        name="synth",
    )(ints, recv, table, radial_matrix())


def grid_kernel(
    ints_ref, sines_ref, recv_ref, vel_ref, t_ref, d_ref, a_ref, out_ref,
    wide, l0e, l0o, l1e, l1o, se, so, ze, zo, ue, uo, oe, oo,
):
    step = pl.program_id(0)

    def widen(u, _):
        row = pl.multiple_of(u * 40, 8)
        wide[pl.ds(row, 16), :] = recv_ref[u, 0].astype(f32)
        wide[pl.ds(row + 16, 16), :] = recv_ref[u, 1].astype(f32)
        return 0

    lax.fori_loop(0, 128, widen, 0, unroll=8)
    for j in range(16):
        for h, zero, one in ((0, l0e, l1e), (1, l0o, l1o)):
            turned = wide[pl.ds(h * 16 + j, 128, stride=40), :].astype(bf16).T
            for k in range(4):
                lanes = slice(128 * k, 128 * k + 128)
                zero[16 * j : 16 * j + 16, lanes] = turned[32 * k : 32 * k + 16]
                one[16 * j : 16 * j + 16, lanes] = turned[32 * k + 16 : 32 * k + 32]
    se[...] = jnp.dot(l1e[...], t_ref[0:512, :], preferred_element_type=f32)
    so[...] = jnp.dot(l1o[...], t_ref[512:1024, :], preferred_element_type=f32)
    ze[...] = jnp.dot(l0e[...], d_ref[0:512, :], preferred_element_type=f32)
    zo[...] = jnp.dot(l0o[...], d_ref[512:1024, :], preferred_element_type=f32)
    south = ints_ref[3]

    def flux(j, _):
        local = jnp.where(south == 1, 15 - j, j)
        sine = sines_ref[step * 16 + j]
        rows = pl.ds(pl.multiple_of(j * 16, 16), 16)
        for b in range(3):
            lo = slice(256 * b, 256 * b + 256)
            hi = slice(NH + 256 * b, NH + 256 * b + 256)
            v0 = vel_ref[0, local, :, lo].astype(f32) * sine
            v1 = vel_ref[1, local, :, lo].astype(f32)
            w0 = vel_ref[0, local, :, hi].astype(f32) * sine
            w1 = vel_ref[1, local, :, hi].astype(f32)
            s_e = se[rows, lo]
            s_o = so[rows, lo]
            z_e = ze[rows, lo]
            z_o = zo[rows, lo]
            near = v0 * (s_e + s_o) + v1 * (z_e + z_o)
            far = w0 * (s_e - s_o) + w1 * (z_e - z_o)
            ue[rows, lo] = (near + far).astype(bf16)
            uo[rows, lo] = (near - far).astype(bf16)
        return 0

    lax.fori_loop(0, 16, flux, 0)
    for dst, src, first in ((oe, ue, 0), (oo, uo, 512)):
        res = lax.dot_general(src[...], a_ref[first : first + 512, :], NT, preferred_element_type=f32)
        for ta in range(4):
            for j in range(16):
                dst[ta, 24 * j : 24 * j + 16, :] = res[16 * j : 16 * j + 16, 128 * ta : 128 * ta + 128]
    for ta in range(4):
        for ip in range(8):
            i0 = pl.ds(2 * ip, 16, stride=24)
            i1 = pl.ds(2 * ip + 1, 16, stride=24)
            parts = swap_chunks(oe[ta, i0, :], oo[ta, i0, :], oe[ta, i1, :], oo[ta, i1, :])
            for al in range(4):
                out_ref[4 * ta + al, :, 128 * ip : 128 * ip + 128] = parts[al].astype(bf16)


def grid_stage(recv, velocity, tables, ints, sines):
    whole = pl.BlockSpec((1024, NH), lambda g, *_: (0, 0), pipeline_mode=pl.Buffered(1))

    def latitude_block(g, ints, sines):
        return (0, jnp.where(ints[3] == 1, 2 - g, g), 0, 0)

    wide = [pltpu.VMEM((256, NH), f32)] * 4
    return pl.pallas_call(
        grid_kernel,
        grid_spec=pltpu.PrefetchScalarGridSpec(
            num_scalar_prefetch=2,
            grid=(3,),
            in_specs=[
                pl.BlockSpec((128, 2, 16, 128), lambda g, *_: (0, 0, g, 0)),
                pl.BlockSpec((2, 16, 16, NLON), latitude_block),
                whole,
                whole,
                whole,
            ],
            out_specs=pl.BlockSpec((16, 16, 1024), lambda g, *_: (0, g, 0)),
            scratch_shapes=[pltpu.VMEM((128 * 40, 128), f32)]
            + [pltpu.VMEM((256, 512), bf16)] * 4
            + wide
            + [pltpu.VMEM((256, NH), bf16)] * 2
            + [pltpu.VMEM((4, 384, 128), f32)] * 2,
        ),
        out_shape=jax.ShapeDtypeStruct((16, 48, 1024), bf16),
        compiler_params=params(),
        cost_estimate=pl.CostEstimate(flops=3700000000, bytes_accessed=14000000, transcendentals=0),
        name="grid",
    )(ints, sines, recv.reshape(128, 2, 48, 128), velocity, *tables)


def analyse_body(par_ref, recv_ref, low_ref, up_ref, out_ref, plus, minus, part_p, part_m):
    step = pl.program_id(0)

    @pl.when(step == 0)
    def _():
        for t in range(8):
            lanes = slice(128 * t, 128 * t + 128)
            for a in range(8):
                north = recv_ref[a, :, lanes].astype(f32)
                south = recv_ref[15 - a, :, lanes].astype(f32)
                part_p[48 * a : 48 * a + 48, :] = north + south
                part_m[48 * a : 48 * a + 48, :] = north - south
            for b in range(3):
                rows = slice(128 * b, 128 * b + 128)
                for part, dst in ((part_p, plus), (part_m, minus)):
                    turned = part[rows, :].T
                    dst[b, 144 * t : 144 * t + 64, :] = turned[0:64]
                    dst[b, 144 * t + 72 : 144 * t + 136, :] = turned[64:128]

    for q in range(2):
        pair = step * 2 + q
        h0 = par_ref[pair]
        for lu in range(2):
            h = h0 if lu == 0 else 1 - h0
            base = h * 32 + q * 16 + step
            left = jnp.concatenate(
                [
                    jnp.concatenate([ref[b, pl.ds(base + 8 * c, 16, stride=72), :] for b in range(3)], 1)
                    for ref in (plus, minus)
                    for c in range(2)
                ],
                0,
            ).astype(bf16)
            table = low_ref[q] if lu == 0 else up_ref[q]
            res = lax.dot_general(left, table, NT, preferred_element_type=f32)
            degree = lax.broadcasted_iota(jnp.int32, (32, res.shape[1]), 1)
            res = jnp.where((degree + h) % 2 == 0, res[0:32], res[32:64]).astype(bf16)
            if lu == 0:
                out_ref[0, q, 0] = res[0:16]
                out_ref[0, q, 1] = res[16:32]
            else:
                zero = jnp.zeros((16, 256), bf16)
                for c in range(2):
                    out_ref[1, q, c, :, 0:256] = zero
                    out_ref[1, q, c, :, 256:512] = res[16 * c : 16 * c + 16]


def analyse(recv, low, up, parity):
    out = pl.BlockSpec((2, 2, 2, 16, LMAX), lambda g, *_: (0, g, 0, 0, 0))
    return pl.pallas_call(
        analyse_body,
        grid_spec=pltpu.PrefetchScalarGridSpec(
            num_scalar_prefetch=1,
            grid=(8,),
            in_specs=[
                pl.BlockSpec((16, 48, 1024), lambda g, *_: (0, 0, 0), pipeline_mode=pl.Buffered(1)),
                pl.BlockSpec((2, LMAX, HALF), lambda g, *_: (g, 0, 0)),
                pl.BlockSpec((2, LMAX // 2, HALF), lambda g, *_: (g, 0, 0)),
            ],
            out_specs=out,
            scratch_shapes=[
                pltpu.VMEM((3, 1152, 128), f32),
                pltpu.VMEM((3, 1152, 128), f32),
                pltpu.VMEM((HALF, 128), f32),
                pltpu.VMEM((HALF, 128), f32),
            ],
        ),
        out_shape=jax.ShapeDtypeStruct((2, 16, 2, 16, LMAX), bf16),
        compiler_params=params(),
        cost_estimate=pl.CostEstimate(flops=1200000000, bytes_accessed=12000000, transcendentals=0),
        name="analyse",
    )(parity, recv, low, up)


def local(source_coeffs, inverses, velocity, order_slots):
    rad_index = lax.axis_index("rad")
    ang_index = lax.axis_index("ang")
    blocks = order_slots.reshape(16, 2, 16)
    lower = blocks[:, 0]
    upper = blocks[:, 1]
    is_even = lower % 2 == 0
    even = jnp.where(is_even, lower, upper)
    odd = jnp.where(is_even, upper, lower)
    by_parity = [v.reshape(16, 8, 2).transpose(2, 0, 1).reshape(256) for v in (even, odd)]
    fourier_orders = jnp.concatenate(by_parity)
    my_orders = lax.dynamic_slice_in_dim(order_slots, ang_index * 32, 32, 0)
    parity = my_orders[:16] % 2
    south = (ang_index >= 8).astype(jnp.int32)
    ints = jnp.concatenate(
        [rad_index[None].astype(jnp.int32), lax.dynamic_slice_in_dim(parity, rad_index * 2, 2, 0), south[None]]
    )
    position = jnp.arange(48, dtype=jnp.int32)
    latitude = ang_index * 48 + jnp.where(south == 1, 47 - position, position)
    sines = jnp.sin((latitude.astype(f32) + 0.5) * (math.pi / NLAT))

    sent = solve(source_coeffs, inverses, my_orders, rad_index)
    coeffs = lax.all_to_all(sent, "rad", 0, 0, tiled=True)
    pairs = [lax.dynamic_slice_in_dim(v, rad_index * 2, 2, 0) for v in (my_orders[:16], my_orders[16:])]
    own_orders = jnp.concatenate(pairs * 2)
    (own,) = legendre_tables(own_orders, ((0, 8, 4, 0),), "legendre_own")
    fields = synth(coeffs, own, ints)
    fields, late, fourier_orders = lax.optimization_barrier((fields, my_orders, fourier_orders))
    fields = lax.all_to_all(fields, ("ang", "rad"), 0, 0, tiled=True)
    low, up = legendre_tables(late, ((0, 16, 16, 0), (16, 16, 16, 8)), "legendre")
    tables = fourier_tables(phase_rows(fourier_orders))
    fields, low, up, tables = lax.optimization_barrier((fields, low, up, tables))
    fourier = grid_stage(fields, velocity, tables, ints, sines)
    fourier = lax.all_to_all(fourier, "ang", 0, 0, tiled=True)
    return analyse(fourier, low, up, parity).reshape(32, 2, 16, LMAX)


def solution(mesh):
    in_specs = (P("ang", "rad", None, None), P("rad", None, None), P(None, "ang", "rad", None), P())
    out_specs = P("ang", None, "rad", None)
    return jax.shard_map(local, mesh=mesh, in_specs=in_specs, out_specs=out_specs, check_vma=False)
```

```python
import functools
import math

import jax
import jax.numpy as jnp
import numpy as np
from jax import lax
from jax.experimental import pallas as pl
from jax.experimental.pallas import tpu as pltpu
from jax.sharding import PartitionSpec as P

f32 = jnp.float32
bf16 = jnp.bfloat16
inner_radius = 0.35
grow_bound = 1e10
grow_log = 23.025850929940457
start_log = -1.2051210046670229
vmem_bytes = 60 * 1024 * 1024

LMAX, NLAT, NLON, NR, K = 512, 768, 1536, 128, 128
HALF = NLAT // 2
NH = NLON // 2
NT = (((1,), (1,)), ((), ()))
TN = (((0,), (0,)), ((), ()))


def radial_matrix():
    u = (np.arange(NR) + 0.5) * (math.pi / NR)
    k = np.arange(K)[:, None]
    r = inner_radius + (1.0 - inner_radius) * (np.cos(u) + 1.0) * 0.5
    value = np.cos(k * u[None])
    slope = k * np.sin(k * u[None]) / np.sin(u)[None] * (2.0 / (1.0 - inner_radius))
    both = np.stack([value / r, slope + 3.0 * value / r], 0)
    both = both.reshape(2, K, 8, 16).transpose(1, 2, 0, 3).reshape(K, 8, 32)
    out = np.zeros((2, K, 8, 2, 32))
    out[0, :, :, 0] = both
    out[1, :, :, 1] = both
    return jnp.asarray(out.reshape(256, 512), f32).astype(bf16)


def params(sem=("arbitrary",)):
    return pltpu.CompilerParams(dimension_semantics=sem, vmem_limit_bytes=vmem_bytes)


def in_vmem(x):
    return pltpu.with_memory_space_constraint(x, pltpu.VMEM)


def swap_chunks(x0, x1, x2, x3):
    lane = lax.broadcasted_iota(jnp.int32, x0.shape, 1)
    low = lane < 64
    even = (lane // 32) % 2 == 0
    a0 = jnp.where(low, x0, pltpu.roll(x2, 64, 1))
    a2 = jnp.where(low, pltpu.roll(x0, 64, 1), x2)
    a1 = jnp.where(low, x1, pltpu.roll(x3, 64, 1))
    a3 = jnp.where(low, pltpu.roll(x1, 64, 1), x3)
    y0 = jnp.where(even, a0, pltpu.roll(a1, 32, 1))
    y1 = jnp.where(even, pltpu.roll(a0, 96, 1), a1)
    y2 = jnp.where(even, a2, pltpu.roll(a3, 32, 1))
    y3 = jnp.where(even, pltpu.roll(a2, 96, 1), a3)
    return (y0, y1, y2, y3)


def solve_kernel(src_ref, inv_ref, out_ref, wide, acc):
    step = pl.program_id(0)
    steps = pl.num_programs(0)
    block = inv_ref.shape[0]

    @pl.when(step == 0)
    def _():
        def widen(s, _):
            wide[pl.ds(pl.multiple_of(s * 136, 8), 128), :] = src_ref[s].astype(f32)
            return 0

        lax.fori_loop(0, 32, widen, 0, unroll=4)

    def degree(i, _):
        row = step * block + i
        x0 = wide[pl.ds(2 * row, 32, stride=136), :]
        x1 = wide[pl.ds(2 * row + 1, 32, stride=136), :]
        x = jnp.concatenate([x0, x1], 0).astype(bf16)
        y = lax.dot_general(x, inv_ref[i], NT, preferred_element_type=f32)
        acc[pl.ds(row, 64, stride=72), :] = y
        return 0

    lax.fori_loop(0, block, degree, 0, unroll=8)

    @pl.when(step == steps - 1)
    def _():
        for r in range(8):
            for lu in range(2):
                for q in range(2):
                    for c in range(2):
                        plane = c * 32 + lu * 16 + 2 * r + q
                        row = (lu * 4 + q * 2 + c) * 64
                        out_ref[r, row : row + 64, :] = acc[plane * 72 : plane * 72 + 64, :].astype(bf16)


def solve(source, inverses):
    return pl.pallas_call(
        solve_kernel,
        grid=(4,),
        in_specs=[
            pl.BlockSpec((32, 128, 128), lambda g: (0, 0, 0)),
            pl.BlockSpec((16, 128, 128), lambda g: (g, 0, 0)),
        ],
        out_specs=pl.BlockSpec((8, 512, 128), lambda g: (0, 0, 0)),
        out_shape=jax.ShapeDtypeStruct((8, 512, 128), bf16),
        scratch_shapes=[pltpu.VMEM((32 * 136, 128), f32), pltpu.VMEM((64 * 72, 128), f32)],
        compiler_params=params(),
        cost_estimate=pl.CostEstimate(flops=134217728, bytes_accessed=4194304, transcendentals=0),
        name="solve",
    )(source.reshape(32, 128, 128), inverses)


def legendre_kernel(groups, c1_ref, c2_ref, m_ref, x_ref, log_ref, *refs):
    outs = refs[: len(groups)]
    p1, p2, lg, bp, tile = refs[len(groups) :]
    step = pl.program_id(0)

    @pl.when(step == 0)
    def _():
        p1[...] = jnp.zeros(p1.shape, f32)
        p2[...] = jnp.zeros(p2.shape, f32)
        bp[...] = jnp.zeros(bp.shape, f32)
        lg[...] = log_ref[...]

    def run(start, count, out_ref):
        rows = slice(start, start + count)
        m = m_ref[rows, :]
        m2 = m * m
        lanes = [slice(128 * t, 128 * t + 128) for t in range(3)]

        def sub(b, state):
            cur, prev, logs, below = state
            scale = [jnp.exp(v) for v in logs]
            for i in range(8):
                local = b * 8 + i
                l = step * 32 + local
                lf = l.astype(f32)
                d = jnp.maximum(lf * lf - m2, 1.0)
                r = lax.rsqrt(d)
                r = r * (1.5 - 0.5 * d * r * r)
                a = c1_ref[l] * r
                ab = a * below
                below = d * r * c2_ref[l]
                seed = jnp.where(m == lf, 1.0, 0.0)
                for t in range(3):
                    new = (a * x_ref[0:count, lanes[t]]) * cur[t] - ab * prev[t] + seed
                    prev[t] = cur[t]
                    cur[t] = new
                    tile[t, pl.ds(local, count, stride=40), :] = new * scale[t]
            for t in range(3):
                big = jnp.abs(cur[t]) > grow_bound
                factor = jnp.where(big, 1.0 / grow_bound, 1.0)
                cur[t] = cur[t] * factor
                prev[t] = prev[t] * factor
                logs[t] = logs[t] + jnp.where(big, grow_log, 0.0)
            return (cur, prev, logs, below)

        state = (
            [p1[rows, v] for v in lanes],
            [p2[rows, v] for v in lanes],
            [lg[rows, v] for v in lanes],
            bp[rows, :],
        )
        cur, prev, logs, below = lax.fori_loop(0, 4, sub, state)
        for t in range(3):
            p1[rows, lanes[t]] = cur[t]
            p2[rows, lanes[t]] = prev[t]
            lg[rows, lanes[t]] = logs[t]
        bp[rows, :] = below
        for s in range(out_ref.shape[0]):
            for t in range(3):
                out_ref[s, :, lanes[t]] = tile[t, s * 40 : s * 40 + 32, :].astype(bf16)

    for (start, count, _, first), out_ref in zip(groups, outs):
        if first == 0:
            run(start, count, out_ref)
        else:
            pl.when(step >= first)(lambda: run(start, count, out_ref))


def legendre_tables(orders, groups, name):
    total = orders.shape[0]
    l = np.arange(LMAX, dtype=np.float64)
    root = np.sqrt(np.maximum(4.0 * l * l - 1.0, 1.0))
    t = (np.arange(HALF) + 0.5) * (math.pi / NLAT)
    gammas = [0.5 * (math.lgamma(m + 1.5) - math.lgamma(m + 1.0)) + start_log for m in range(LMAX)]
    x = jnp.asarray(np.broadcast_to(np.cos(t), (16, HALF)), f32)
    mf = orders.astype(f32)
    logs = jnp.take(jnp.asarray(gammas, f32), orders)[:, None] + mf[:, None] * jnp.asarray(np.log(np.sin(t)), f32)[None]

    def out_spec(slots, first):
        return pl.BlockSpec((slots, 32, HALF), lambda g, *_: (0, jnp.maximum(g - first, 0), 0))

    return pl.pallas_call(
        functools.partial(legendre_kernel, groups),
        grid_spec=pltpu.PrefetchScalarGridSpec(
            num_scalar_prefetch=2,
            grid=(16,),
            in_specs=[
                pl.BlockSpec((total, 128), lambda g, *_: (0, 0)),
                pl.BlockSpec((16, HALF), lambda g, *_: (0, 0)),
                pl.BlockSpec((total, HALF), lambda g, *_: (0, 0)),
            ],
            out_specs=[out_spec(slots, first) for _, _, slots, first in groups],
            scratch_shapes=[
                pltpu.VMEM((total, HALF), f32),
                pltpu.VMEM((total, HALF), f32),
                pltpu.VMEM((total, HALF), f32),
                pltpu.VMEM((total, 128), f32),
                pltpu.VMEM((3, 640, 128), f32),
            ],
        ),
        out_shape=[jax.ShapeDtypeStruct((slots, LMAX - 32 * first, HALF), bf16) for _, _, slots, first in groups],
        compiler_params=params(),
        cost_estimate=pl.CostEstimate(flops=2000000 * total, bytes_accessed=400000 * total, transcendentals=3000 * total),
        name=name,
    )(
        jnp.asarray(root, f32),
        jnp.asarray(1.0 / root, f32),
        jnp.broadcast_to(mf[:, None], (total, 128)),
        x,
        logs,
    )


def phase_rows(orders):
    m = orders[:, None]
    near = (m * jnp.arange(128, dtype=jnp.int32)[None]) % NLON
    far = (m * (128 * jnp.arange(8, dtype=jnp.int32))[None]) % NLON
    near = near.astype(f32) * (2.0 * math.pi / NLON)
    far = far.astype(f32) * (2.0 * math.pi / NLON)
    m = orders.astype(f32)
    w = jnp.where(m == 0.0, 1.0, 2.0)
    weights = jnp.stack([w, -m * w] * 4, 1)
    return (jnp.cos(near), jnp.sin(near), jnp.cos(far), jnp.sin(far), weights)


def table_kernel(nc, ns, fc, fs, w, t_ref, d_ref, a_ref):
    scale = (2.0 * math.pi / NLON) * (math.pi / NLAT)
    for b in range(6):
        lanes = slice(128 * b, 128 * b + 128)
        parts = []
        for q in range(2):
            rows = slice(128 * q, 128 * q + 128)
            far_cos = fc[rows, b : b + 1]
            far_sin = fs[rows, b : b + 1]
            cosine = far_cos * nc[rows, :] - far_sin * ns[rows, :]
            sine = far_sin * nc[rows, :] + far_cos * ns[rows, :]
            weight = w[rows, 0:1]
            turn = w[rows, 1:2]
            first = slice(256 * q, 256 * q + 128)
            second = slice(256 * q + 128, 256 * q + 256)
            t_ref[first, lanes] = (weight * cosine).astype(bf16)
            t_ref[second, lanes] = (-weight * sine).astype(bf16)
            d_ref[first, lanes] = (turn * sine).astype(bf16)
            d_ref[second, lanes] = (turn * cosine).astype(bf16)
            parts += [scale * cosine, -scale * sine]
        for a in range(16):
            rows = jnp.concatenate([v[8 * a : 8 * a + 8] for v in parts], 0)
            a_ref[32 * a : 32 * a + 32, lanes] = rows.astype(bf16)


def fourier_tables(rows):
    near = pl.BlockSpec((256, 128), lambda g: (g, 0))
    far = pl.BlockSpec((256, 8), lambda g: (g, 0))
    out = pl.BlockSpec((512, NH), lambda g: (g, 0))
    return pl.pallas_call(
        table_kernel,
        grid=(2,),
        in_specs=[near, near, far, far, far],
        out_specs=[out, out, out],
        out_shape=[jax.ShapeDtypeStruct((1024, NH), bf16)] * 3,
        compiler_params=params(),
        cost_estimate=pl.CostEstimate(flops=8000000, bytes_accessed=8000000, transcendentals=0),
        name="tables",
    )(*rows)


def synth_kernel(ints_ref, recv_ref, leg_ref, mat_ref, out_ref, ns):
    mat = mat_ref[...]
    for lu in range(2):
        for q in range(2):
            first = 4 * lu
            count = 64 * (8 - first)
            h = ints_ref[1 + q]
            h = h if lu == 0 else 1 - h
            planes = []
            for c in range(2):
                row = (lu * 4 + q * 2 + c) * 64
                planes.append(recv_ref[first:8, row : row + 64, :].reshape(count, 128))
            coeffs = jnp.concatenate(planes, 1)
            rad = jnp.dot(coeffs, mat, preferred_element_type=f32)
            degree = lax.broadcasted_iota(jnp.int32, rad.shape, 0) + 64 * first
            rad = jnp.where(degree >= ints_ref[4 + 2 * lu + q], rad, 0.0)
            sign = (1 - 2 * ((degree + h) % 2)).astype(f32)
            both = jnp.concatenate([rad.astype(bf16), (rad * sign).astype(bf16)], 1)
            table = leg_ref[lu * 2 + q, 64 * first : LMAX, :]
            wave = lax.dot_general(table, both, TN, preferred_element_type=f32)
            for tile in range(8):
                ns[lu * 2 + q, tile] = wave[:, 128 * tile : 128 * tile + 128]
    low = lax.broadcasted_iota(jnp.int32, (HALF, 128), 1) < 64
    for h in range(2):
        first, second = [(ints_ref[1 + q] if h == 0 else 1 - ints_ref[1 + q]) * 2 + q for q in range(2)]
        for half in range(2):
            for rh in range(4):
                v0 = ns[first, half * 4 + rh]
                v1 = ns[second, half * 4 + rh]
                parts = (
                    jnp.where(low, v0, pltpu.roll(v1, 64, 1)),
                    jnp.where(low, pltpu.roll(v0, 64, 1), v1),
                )
                for rl in range(2):
                    for north in range(8):
                        a = north if half == 0 else 15 - north
                        rows = parts[rl][48 * north : 48 * north + 48]
                        out_ref[a * 8 + rh * 2 + rl, 48 * h : 48 * h + 48, :] = rows.astype(bf16)


def synth(recv, table, ints):
    return pl.pallas_call(
        synth_kernel,
        grid_spec=pltpu.PrefetchScalarGridSpec(
            num_scalar_prefetch=1,
            grid=(1,),
            in_specs=[
                pl.BlockSpec(memory_space=pltpu.VMEM),
                pl.BlockSpec((4, LMAX, HALF), lambda g, b: (0, 0, 0)),
                pl.BlockSpec((256, 512), lambda g, b: (0, 0)),
            ],
            out_specs=pl.BlockSpec((128, 96, 128), lambda g, b: (0, 0, 0)),
            scratch_shapes=[pltpu.VMEM((4, 8, HALF, 128), f32)],
        ),
        out_shape=jax.ShapeDtypeStruct((128, 96, 128), bf16),
        compiler_params=params(),
        cost_estimate=pl.CostEstimate(flops=2000000000, bytes_accessed=7000000, transcendentals=0),
        name="synth",
    )(ints, in_vmem(recv), table, radial_matrix())


def grid_kernel(
    ints_ref, sines_ref, recv_ref, vel_ref, t_ref, d_ref, a_ref, out_ref,
    wide, l0e, l0o, l1e, l1o, se, so, ze, zo, ue, uo, oe, oo,
):
    step = pl.program_id(0)
    now = pl.ds(pl.multiple_of(step * 16, 16), 16)

    def widen(u, _):
        row = pl.multiple_of(u * 40, 8)
        wide[pl.ds(row, 16), :] = recv_ref[u, 0, now, :].astype(f32)
        wide[pl.ds(row + 16, 16), :] = recv_ref[u, 1, now, :].astype(f32)
        return 0

    lax.fori_loop(0, 128, widen, 0, unroll=8)
    for j in range(16):
        for h, zero, one in ((0, l0e, l1e), (1, l0o, l1o)):
            turned = wide[pl.ds(h * 16 + j, 128, stride=40), :].astype(bf16).T
            for k in range(4):
                lanes = slice(128 * k, 128 * k + 128)
                zero[16 * j : 16 * j + 16, lanes] = turned[32 * k : 32 * k + 16]
                one[16 * j : 16 * j + 16, lanes] = turned[32 * k + 16 : 32 * k + 32]
    se[...] = jnp.dot(l1e[...], t_ref[0:512, :], preferred_element_type=f32)
    so[...] = jnp.dot(l1o[...], t_ref[512:1024, :], preferred_element_type=f32)
    ze[...] = jnp.dot(l0e[...], d_ref[0:512, :], preferred_element_type=f32)
    zo[...] = jnp.dot(l0o[...], d_ref[512:1024, :], preferred_element_type=f32)
    south = ints_ref[3]

    def flux(j, _):
        local = jnp.where(south == 1, 15 - j, j)
        sine = sines_ref[step * 16 + j]
        rows = pl.ds(pl.multiple_of(j * 16, 16), 16)
        for b in range(3):
            lo = slice(256 * b, 256 * b + 256)
            hi = slice(NH + 256 * b, NH + 256 * b + 256)
            v0 = vel_ref[0, local, :, lo].astype(f32) * sine
            v1 = vel_ref[1, local, :, lo].astype(f32)
            w0 = vel_ref[0, local, :, hi].astype(f32) * sine
            w1 = vel_ref[1, local, :, hi].astype(f32)
            s_e = se[rows, lo]
            s_o = so[rows, lo]
            z_e = ze[rows, lo]
            z_o = zo[rows, lo]
            near = v0 * (s_e + s_o) + v1 * (z_e + z_o)
            far = w0 * (s_e - s_o) + w1 * (z_e - z_o)
            ue[rows, lo] = (near + far).astype(bf16)
            uo[rows, lo] = (near - far).astype(bf16)
        return 0

    lax.fori_loop(0, 16, flux, 0)
    for dst, src, first in ((oe, ue, 0), (oo, uo, 512)):
        res = lax.dot_general(src[...], a_ref[first : first + 512, :], NT, preferred_element_type=f32)
        for ta in range(4):
            for j in range(16):
                dst[ta, 24 * j : 24 * j + 16, :] = res[16 * j : 16 * j + 16, 128 * ta : 128 * ta + 128]
    for ta in range(4):
        for ip in range(8):
            i0 = pl.ds(2 * ip, 16, stride=24)
            i1 = pl.ds(2 * ip + 1, 16, stride=24)
            parts = swap_chunks(oe[ta, i0, :], oo[ta, i0, :], oe[ta, i1, :], oo[ta, i1, :])
            for al in range(4):
                out_ref[4 * ta + al, :, 128 * ip : 128 * ip + 128] = parts[al].astype(bf16)


def grid_stage(recv, velocity, tables, ints, sines):
    whole = pl.BlockSpec((1024, NH), lambda g, *_: (0, 0), pipeline_mode=pl.Buffered(1))

    def latitude_block(g, ints, sines):
        return (0, jnp.where(ints[3] == 1, 2 - g, g), 0, 0)

    wide = [pltpu.VMEM((256, NH), f32)] * 4
    return pl.pallas_call(
        grid_kernel,
        grid_spec=pltpu.PrefetchScalarGridSpec(
            num_scalar_prefetch=2,
            grid=(3,),
            in_specs=[
                pl.BlockSpec(memory_space=pltpu.VMEM),
                pl.BlockSpec((2, 16, 16, NLON), latitude_block),
                whole,
                whole,
                whole,
            ],
            out_specs=pl.BlockSpec((16, 16, 1024), lambda g, *_: (0, g, 0)),
            scratch_shapes=[pltpu.VMEM((128 * 40, 128), f32)]
            + [pltpu.VMEM((256, 512), bf16)] * 4
            + wide
            + [pltpu.VMEM((256, NH), bf16)] * 2
            + [pltpu.VMEM((4, 384, 128), f32)] * 2,
        ),
        out_shape=jax.ShapeDtypeStruct((16, 48, 1024), bf16),
        compiler_params=params(),
        cost_estimate=pl.CostEstimate(flops=3700000000, bytes_accessed=14000000, transcendentals=0),
        name="grid",
    )(ints, sines, in_vmem(recv.reshape(128, 2, 48, 128)), velocity, *tables)


def analyse_body(par_ref, recv_ref, low_ref, up_ref, out_ref, plus, minus, part_p, part_m):
    step = pl.program_id(0)

    @pl.when(step == 0)
    def _():
        for t in range(8):
            lanes = slice(128 * t, 128 * t + 128)
            for a in range(8):
                north = recv_ref[a, :, lanes].astype(f32)
                south = recv_ref[15 - a, :, lanes].astype(f32)
                part_p[48 * a : 48 * a + 48, :] = north + south
                part_m[48 * a : 48 * a + 48, :] = north - south
            for b in range(3):
                rows = slice(128 * b, 128 * b + 128)
                for part, dst in ((part_p, plus), (part_m, minus)):
                    turned = part[rows, :].astype(bf16).T.astype(f32)
                    dst[b, 144 * t : 144 * t + 64, :] = turned[0:64]
                    dst[b, 144 * t + 72 : 144 * t + 136, :] = turned[64:128]

    for q in range(4):
        pair = step * 4 + q
        h0 = par_ref[pair]
        for lu in range(2):
            h = h0 if lu == 0 else 1 - h0
            base = h * 32 + (q % 2) * 16 + step * 2 + q // 2
            left = jnp.concatenate(
                [
                    jnp.concatenate([ref[b, pl.ds(base + 8 * c, 16, stride=72), :] for b in range(3)], 1)
                    for ref in (plus, minus)
                    for c in range(2)
                ],
                0,
            ).astype(bf16)
            table = low_ref[q] if lu == 0 else up_ref[q]
            res = lax.dot_general(left, table, NT, preferred_element_type=f32)
            degree = lax.broadcasted_iota(jnp.int32, (32, res.shape[1]), 1)
            res = jnp.where((degree + h) % 2 == 0, res[0:32], res[32:64]).astype(bf16)
            if lu == 0:
                out_ref[0, q, 0] = res[0:16]
                out_ref[0, q, 1] = res[16:32]
            else:
                zero = jnp.zeros((16, 256), bf16)
                for c in range(2):
                    out_ref[1, q, c, :, 0:256] = zero
                    out_ref[1, q, c, :, 256:512] = res[16 * c : 16 * c + 16]


def analyse(recv, low, up, parity):
    out = pl.BlockSpec((2, 4, 2, 16, LMAX), lambda g, *_: (0, g, 0, 0, 0))
    return pl.pallas_call(
        analyse_body,
        grid_spec=pltpu.PrefetchScalarGridSpec(
            num_scalar_prefetch=1,
            grid=(4,),
            in_specs=[
                pl.BlockSpec((16, 48, 1024), lambda g, *_: (0, 0, 0), pipeline_mode=pl.Buffered(1)),
                pl.BlockSpec((4, LMAX, HALF), lambda g, *_: (g, 0, 0)),
                pl.BlockSpec((4, LMAX // 2, HALF), lambda g, *_: (g, 0, 0)),
            ],
            out_specs=out,
            scratch_shapes=[
                pltpu.VMEM((3, 1152, 128), f32),
                pltpu.VMEM((3, 1152, 128), f32),
                pltpu.VMEM((HALF, 128), f32),
                pltpu.VMEM((HALF, 128), f32),
            ],
        ),
        out_shape=jax.ShapeDtypeStruct((2, 16, 2, 16, LMAX), bf16),
        compiler_params=params(),
        cost_estimate=pl.CostEstimate(flops=1200000000, bytes_accessed=12000000, transcendentals=0),
        name="analyse",
    )(parity, recv, low, up)


def local(source_coeffs, inverses, velocity, order_slots):
    rad_index = lax.axis_index("rad")
    ang_index = lax.axis_index("ang")
    blocks = order_slots.reshape(16, 2, 16)
    lower = blocks[:, 0]
    upper = blocks[:, 1]
    is_even = lower % 2 == 0
    even = jnp.where(is_even, lower, upper)
    odd = jnp.where(is_even, upper, lower)
    by_parity = [v.reshape(16, 8, 2).transpose(2, 0, 1).reshape(256) for v in (even, odd)]
    fourier_orders = jnp.concatenate(by_parity)
    my_orders = lax.dynamic_slice_in_dim(order_slots, ang_index * 32, 32, 0)
    parity = my_orders[:16] % 2
    pairs = [lax.dynamic_slice_in_dim(v, rad_index * 2, 2, 0) for v in (my_orders[:16], my_orders[16:])]
    own_orders = jnp.concatenate(pairs * 2)
    south = (ang_index >= 8).astype(jnp.int32)
    ints = jnp.concatenate(
        [rad_index[None].astype(jnp.int32), lax.dynamic_slice_in_dim(parity, rad_index * 2, 2, 0), south[None], own_orders[:4]]
    )
    position = jnp.arange(48, dtype=jnp.int32)
    latitude = ang_index * 48 + jnp.where(south == 1, 47 - position, position)
    sines = jnp.sin((latitude.astype(f32) + 0.5) * (math.pi / NLAT))

    sent = solve(source_coeffs, inverses)
    coeffs = lax.all_to_all(sent, "rad", 0, 0, tiled=True)
    (own,) = legendre_tables(own_orders, ((0, 8, 4, 0),), "legendre_own")
    fields = synth(coeffs, own, ints)
    fields, late, fourier_orders = lax.optimization_barrier((fields, my_orders, fourier_orders))
    fields = lax.all_to_all(fields, ("ang", "rad"), 0, 0, tiled=True)
    low, up = legendre_tables(late, ((0, 16, 16, 0), (16, 16, 16, 8)), "legendre")
    tables = fourier_tables(phase_rows(fourier_orders))
    fields, low, up, tables = lax.optimization_barrier((fields, low, up, tables))
    fourier = grid_stage(fields, velocity, tables, ints, sines)
    fourier = lax.all_to_all(fourier, "ang", 0, 0, tiled=True)
    return analyse(fourier, low, up, parity).reshape(32, 2, 16, LMAX)


def solution(mesh):
    in_specs = (P("ang", "rad", None, None), P("rad", None, None), P(None, "ang", "rad", None), P())
    out_specs = P("ang", None, "rad", None)
    return jax.shard_map(local, mesh=mesh, in_specs=in_specs, out_specs=out_specs, check_vma=False)
```
